256 devices in a mesh: frames: 32 (over y, z), codes: 8 (over x, core).
Axes of the slice: x: 4, y: 4, z: 8, core: 2. Of those that a mesh axis runs over, the one named last changes fastest.
Arguments:
- frames: bfloat16 [262144, 256], P(('frames', 'codes')), may hold values from -32 to 32
- codes: bfloat16 [65536, 256], P('codes'), may hold values from -2 to 2
- pattern: int32 [2048, 48], P('frames'), may hold values from 0 to 512, as said below
Outputs:
- row_potential: float32 [262144], P('frames')
- col_potential: float32 [65536], P('codes')
The draws below stay inside these ranges and needn't reach their ends.
Inputs may be any that keep to these rules, and one draw needn't show every extreme that they name: `pattern`: each row lists distinct code blocks in increasing order, padded at its end with 512; it lists at least one block, and at most 6 of the 64 blocks k*64 to (k+1)*64 - 1 of any group k, exactly 6 in some row; every code block is listed by some row.
All inputs are finite; a program needn't handle non-finite values.
Results may differ from the reference program's by a relative error of at most 0.0046.
Values may be sent and summed in bfloat16 or wider, within the bound.
No kernel may reach another device: no remote copies, remote signals or barrier semaphores. Data moves between devices by JAX's collectives and lax.ppermute only.
A program may use at most 128 MiB of HBM per device.

```python
import math
import jax
import jax.numpy as jnp
from jax import lax

W = 256
K = 65536
BLK = 128
GB = 64
CAP = 6
ITERS = 3
NFB = 2048
F = 262144
NCB = 512
SLOTS = 48


def code_table(key):
    base_key = jax.random.fold_in(key, 101)
    code_rows = jax.random.normal(jax.random.fold_in(base_key, 1), (K, W), jnp.float32) / math.sqrt(W)
    return jnp.clip(code_rows, -2.0, 2.0)


def draw_codes(key, part):
    return code_table(key).astype(jnp.bfloat16)


def draw_frames(key, part):
    base_key = jax.random.fold_in(key, 202)
    frame_rows = jax.random.normal(jax.random.fold_in(base_key, 1), (NFB * BLK, W), jnp.float32)
    return jnp.clip(frame_rows, -32.0, 32.0).astype(jnp.bfloat16)


def draw_pattern(key, part):
    base_key = jax.random.fold_in(key, 303)
    groups = NCB // GB
    stride = min(NFB, NCB)
    block_ids = jnp.arange(NFB, dtype=jnp.int32)
    code_ids = jnp.arange(NCB, dtype=jnp.int32)
    counts = jax.random.randint(jax.random.fold_in(base_key, 1), (NFB, groups), 1, CAP + 1)
    forced = (code_ids[None, :] - block_ids[:, None]) % stride == 0
    forced_groups = jnp.max(forced.reshape(NFB, groups, GB).astype(jnp.int32), axis=2)
    counts = jnp.maximum(counts, forced_groups)
    counts = counts.at[NFB - 1, 0].set(CAP)
    scores = jax.random.randint(jax.random.fold_in(base_key, 2), (NFB, NCB), 0, 1 << 20) * GB + (code_ids % GB)[None, :]
    scores = jnp.where(forced, -1, scores)
    grouped = scores.reshape(NFB, groups, GB)
    rank_in_group = jnp.sum((grouped[:, :, None, :] < grouped[:, :, :, None]).astype(jnp.int32), axis=3)
    chosen = (rank_in_group < counts[:, :, None]).reshape(NFB, NCB)
    sort_keys = jnp.where(chosen, code_ids[None, :], NCB + code_ids[None, :])
    ordered = jnp.sort(sort_keys, axis=1)[:, :SLOTS]
    return jnp.where(ordered < NCB, ordered, NCB).astype(jnp.int32)


def setup_inputs(seed: int = 0) -> dict:
    keys = jax.random.split(jax.random.key(seed), 4)
    frames = draw_frames(jax.random.fold_in(keys[3], 71), 0)
    codes = draw_codes(jax.random.fold_in(keys[3], 71), 0)
    pattern = draw_pattern(jax.random.fold_in(keys[3], 71), 0)
    return {"frames": frames, "codes": codes, "pattern": pattern}


NEG_FILL = -1e30
LOGIT_SCALE = 2.0


def tile_logits(frames, codes, pattern):
    frame_blocks = frames.reshape(NFB, BLK, W)
    code_blocks = codes.reshape(NCB, BLK, W)

    def one_block(inputs):
        block_rows, picked = inputs
        chosen = code_blocks[jnp.minimum(picked, NCB - 1)]
        product = jnp.einsum("iw,sjw->sij", block_rows.astype(jnp.float32), chosen.astype(jnp.float32), precision=lax.Precision.HIGHEST)
        return (product * LOGIT_SCALE).astype(jnp.bfloat16)

    return lax.map(one_block, (frame_blocks, pattern))


def row_pass(logits, usable, pattern, col_potential):
    col_blocks = col_potential.reshape(NCB, BLK)

    def one_block(inputs):
        block_tiles, block_mask, picked = inputs
        row_shift = col_blocks[jnp.minimum(picked, NCB - 1)]
        scores = block_tiles.astype(jnp.float32) + row_shift[:, None, :]
        scores = jnp.where(block_mask[:, None, None], scores, NEG_FILL)
        highest = jnp.max(scores, axis=(0, 2))
        exp_terms = jnp.exp(scores - highest[None, :, None])
        summed = jnp.sum(jnp.where(block_mask[:, None, None], exp_terms, 0.0), axis=(0, 2))
        return -(highest + jnp.log(summed))

    return lax.map(one_block, (logits, usable, pattern)).reshape(-1)


def column_pass(logits, usable, pattern, row_potential):
    row_blocks = row_potential.reshape(NFB, BLK)

    def block_max(inputs):
        block_tiles, block_mask, row_shift = inputs
        scores = block_tiles.astype(jnp.float32) + row_shift[None, :, None]
        scores = jnp.where(block_mask[:, None, None], scores, NEG_FILL)
        return jnp.max(scores, axis=1)

    tile_high = lax.map(block_max, (logits, usable, row_blocks))
    highest = jnp.full((NCB + 1, BLK), NEG_FILL, jnp.float32).at[pattern].max(tile_high)

    def block_sum(inputs):
        block_tiles, block_mask, row_shift, picked = inputs
        scores = block_tiles.astype(jnp.float32) + row_shift[None, :, None]
        exp_terms = jnp.exp(scores - highest[picked][:, None, :])
        return jnp.sum(jnp.where(block_mask[:, None, None], exp_terms, 0.0), axis=1)

    tile_sum = lax.map(block_sum, (logits, usable, row_blocks, pattern))
    summed = jnp.zeros((NCB + 1, BLK), jnp.float32).at[pattern].add(tile_sum)
    log_ratio = math.log(F / K)
    return (log_ratio - (highest[:NCB] + jnp.log(summed[:NCB]))).reshape(-1)


def reference(frames, codes, pattern):
    logits = tile_logits(frames, codes, pattern)
    usable = pattern < NCB
    col_potential = jnp.zeros((K,), jnp.float32)
    row_potential = jnp.zeros((F,), jnp.float32)
    for iteration in range(ITERS):
        row_potential = row_pass(logits, usable, pattern, col_potential)
        col_potential = column_pass(logits, usable, pattern, row_potential)
    return row_potential, col_potential
```

```python
import functools
import math

import jax
import jax.numpy as jnp
from jax import lax
from jax.experimental import pallas as pl
from jax.experimental.pallas import tpu as pltpu
from jax.sharding import Mesh
from jax.sharding import PartitionSpec as P

BLK = 128
GB = 64
CAP = 6
ITERS = 3
PER = 8
CODES = ("codes_0", "codes_1")
FRAMES = ("frames_0", "frames_1")
FRAMES_CODES = ("frames_0", "frames_1", "codes_0", "codes_1")

NEG_FILL = -1e30
NEG_ROW = -1e29
SMALL = 1e-26
VMEM = 56 * 1024 * 1024


def tiles_kernel(picks, frames_ref, codes_ref, exp_ref, logit_ref, high_ref, lse_ref):
    group = pl.program_id(0)
    for b in range(PER):
        lanes = slice(b * BLK, (b + 1) * BLK)
        block = frames_ref[lanes, :] * jnp.bfloat16(2.0)
        top = None
        for s in range(CAP):
            pick = picks[(group * PER + b) * 8 + s]
            chosen = codes_ref[jnp.maximum(pick, 0)]
            tile = lax.dot_general(
                chosen, block, (((1,), (1,)), ((), ())), preferred_element_type=jnp.float32
            )
            tile = jnp.where(pick >= 0, tile, NEG_FILL).astype(jnp.bfloat16)
            logit_ref[0, s * BLK : (s + 1) * BLK, lanes] = tile
            part = jnp.max(tile.astype(jnp.float32).reshape(BLK // 8, 8, BLK), axis=0)
            top = part if top is None else jnp.maximum(top, part)
        high = jnp.maximum(jnp.max(top, axis=0, keepdims=True), NEG_ROW)
        total = None
        for s in range(CAP):
            tile = logit_ref[0, s * BLK : (s + 1) * BLK, lanes].astype(jnp.float32)
            terms = jnp.exp(tile - high)
            exp_ref[0, s * BLK : (s + 1) * BLK, lanes] = terms.astype(jnp.bfloat16)
            part = jnp.sum(terms.reshape(BLK // 8, 8, BLK), axis=0)
            total = part if total is None else total + part
        total = jnp.sum(total, axis=0, keepdims=True)
        high_ref[b : b + 1, :] = high
        lse_ref[b : b + 1, :] = jnp.where(total > 0.0, high + jnp.log(total), NEG_FILL)


def make_tiles(picks, frames, codes):
    groups = frames.shape[0] // (PER * BLK)
    rows = groups * PER
    return pl.pallas_call(
        tiles_kernel,
        grid_spec=pltpu.PrefetchScalarGridSpec(
            num_scalar_prefetch=1,
            grid=(groups,),
            in_specs=[
                pl.BlockSpec((PER * BLK, frames.shape[1]), lambda g, _: (g, 0)),
                pl.BlockSpec(codes.shape, lambda g, _: (0, 0, 0), pipeline_mode=pl.Buffered(1)),
            ],
            out_specs=[
                pl.BlockSpec((1, CAP * BLK, PER * BLK), lambda g, _: (g, 0, 0)),
                pl.BlockSpec((1, CAP * BLK, PER * BLK), lambda g, _: (g, 0, 0)),
                pl.BlockSpec((PER, BLK), lambda g, _: (g, 0)),
                pl.BlockSpec((PER, BLK), lambda g, _: (g, 0)),
            ],
        ),
        out_shape=[
            jax.ShapeDtypeStruct((groups, CAP * BLK, PER * BLK), jnp.bfloat16),
            jax.ShapeDtypeStruct((groups, CAP * BLK, PER * BLK), jnp.bfloat16),
            jax.ShapeDtypeStruct((rows, BLK), jnp.float32),
            jax.ShapeDtypeStruct((rows, BLK), jnp.float32),
        ],
        compiler_params=pltpu.CompilerParams(vmem_limit_bytes=VMEM),
        name="make_tiles",
    )(picks, frames, codes)


def log_sum(pieces_ref):
    count = pieces_ref.shape[0]
    high = pieces_ref[0]
    for k in range(1, count):
        high = jnp.maximum(high, pieces_ref[k])
    total = jnp.exp(pieces_ref[0] - high)
    for k in range(1, count):
        total = total + jnp.exp(pieces_ref[k] - high)
    return high + jnp.log(total)


def split_dot(selector, values):
    upper = values.astype(jnp.bfloat16)
    lower = (values - upper.astype(jnp.float32)).astype(jnp.bfloat16)
    return jnp.dot(selector, upper, preferred_element_type=jnp.float32) + jnp.dot(
        selector, lower, preferred_element_type=jnp.float32
    )


def stable_pass(picks, logit_ref, shift_ref, out_ref, block_ref, high_ref, total_ref, by_code):
    high_ref[...] = jnp.full_like(high_ref, NEG_FILL)
    total_ref[...] = jnp.zeros_like(total_ref)

    def one_group(g, _):
        pltpu.sync_copy(logit_ref.at[g], block_ref)

        def one_tile(index, _):
            b = index // CAP
            s = index - b * CAP
            row = g * PER + b
            pick = picks[row * 8 + s]

            @pl.when(pick >= 0)
            def _():
                rows = pl.ds(pl.multiple_of(s * BLK, BLK), BLK)
                lanes = pl.ds(pl.multiple_of(b * BLK, BLK), BLK)
                tile = block_ref[rows, lanes].astype(jnp.float32)
                if by_code:
                    tile = jnp.transpose(tile + shift_ref[pl.ds(row, 1), :])
                    at = pl.ds(pick, 1)
                else:
                    shift = jnp.broadcast_to(shift_ref[pl.ds(pick, 1), :], (BLK, BLK))
                    tile = tile + jnp.transpose(shift)
                    at = pl.ds(row, 1)
                before = high_ref[at, :]
                high = jnp.maximum(before, jnp.max(tile, axis=0, keepdims=True))
                total_ref[at, :] = total_ref[at, :] * jnp.exp(before - high) + jnp.sum(
                    jnp.exp(tile - high), axis=0, keepdims=True
                )
                high_ref[at, :] = high

            return 0

        lax.fori_loop(0, CAP * PER, one_tile, 0)
        return 0

    lax.fori_loop(0, logit_ref.shape[0], one_group, 0)
    total = total_ref[...]
    out_ref[...] = jnp.where(
        total > 0.0, high_ref[...] + jnp.log(jnp.maximum(total, 1e-37)), NEG_FILL
    )


def column_kernel(
    copies, picks, pieces_ref, high_ref, picks_ref, exp_ref, logit_ref, row_ref, out_ref,
    scale_ref, sums_ref, peak_ref, lse_ref, block_ref, top_ref, total_ref,
):
    group = pl.program_id(0)

    @pl.when(group == 0)
    def _():
        row = -log_sum(pieces_ref)
        row_ref[...] = row
        weight = high_ref[...] + row
        peak = jnp.max(weight)
        peak_ref[0] = peak
        scale_ref[...] = jnp.exp(weight - peak)

    scale = scale_ref[pl.ds(pl.multiple_of(group * PER, PER), PER), :]
    wide = jnp.concatenate([scale] * PER, axis=1)
    lane_block = lax.broadcasted_iota(jnp.int32, wide.shape, 1) // BLK
    row_block = lax.broadcasted_iota(jnp.int32, wide.shape, 0)
    wide = jnp.where(lane_block == row_block, wide, 0.0).astype(jnp.bfloat16)
    sums_ref[pl.ds(pl.multiple_of(group * PER, PER), PER), :] = lax.dot_general(
        wide, exp_ref[0], (((1,), (1,)), ((), ())), preferred_element_type=jnp.float32
    )

    @pl.when(group == pl.num_programs(0) - 1)
    def _():
        blocks = lax.broadcasted_iota(jnp.int32, (GB, picks_ref.shape[1]), 0)
        total = jnp.zeros(lse_ref.shape, jnp.float32)
        used = jnp.zeros((GB, 1), jnp.float32)
        for s in range(CAP):
            hit = (picks_ref[s : s + 1, :] == blocks).astype(jnp.float32)
            used = used + jnp.sum(hit, axis=1, keepdims=True)
            total = total + split_dot(
                hit.astype(jnp.bfloat16), sums_ref[:, s * BLK : (s + 1) * BLK]
            )
        lse_ref[...] = jnp.where(
            total > 0.0, peak_ref[0] + jnp.log(jnp.maximum(total, 1e-37)), NEG_FILL
        )
        low = jnp.min(jnp.where(used > 0.0, total, 1.0))

        @pl.when(jnp.logical_not(low >= SMALL))
        def _():
            stable_pass(
                picks, logit_ref, row_ref, lse_ref, block_ref, top_ref, total_ref, True
            )

        for k in range(copies):
            out_ref[k] = lse_ref[...]


def row_kernel(
    copies, log_ratio, picks, pieces_ref, high_ref, picks_ref, exp_ref, logit_ref, out_ref,
    col_ref, scale_ref, sums_ref, peak_ref, lse_ref, block_ref, top_ref, total_ref,
):
    group = pl.program_id(0)

    @pl.when(group == 0)
    def _():
        col = log_ratio - log_sum(pieces_ref)
        col_ref[...] = col
        peak = jnp.max(col)
        peak_ref[0] = peak
        scale = jnp.exp(col - peak).astype(jnp.bfloat16)
        blocks = lax.broadcasted_iota(jnp.int32, (picks_ref.shape[0], GB), 1)
        for s in range(CAP):
            hit = (picks_ref[:, s : s + 1] == blocks).astype(jnp.float32).astype(jnp.bfloat16)
            scale_ref[:, s * BLK : (s + 1) * BLK] = jnp.dot(
                hit, scale, preferred_element_type=jnp.float32
            )

    at = pl.ds(pl.multiple_of(group * PER, PER), PER)
    scale = scale_ref[at, :].astype(jnp.bfloat16)
    wide = jnp.dot(scale, exp_ref[0], preferred_element_type=jnp.float32)
    row_block = lax.broadcasted_iota(jnp.int32, (PER, BLK), 0)
    total = jnp.zeros((PER, BLK), jnp.float32)
    for b in range(PER):
        total = total + jnp.where(row_block == b, wide[:, b * BLK : (b + 1) * BLK], 0.0)
    sums_ref[at, :] = total

    @pl.when(group == pl.num_programs(0) - 1)
    def _():
        total = sums_ref[...]
        lse_ref[...] = jnp.where(
            total > 0.0,
            high_ref[...] + (peak_ref[0] + jnp.log(jnp.maximum(total, 1e-37))),
            NEG_FILL,
        )
        low = jnp.min(jnp.where(picks_ref[:, 0:1] >= 0, total, 1.0))

        @pl.when(jnp.logical_not(low >= SMALL))
        def _():
            stable_pass(
                picks, logit_ref, col_ref, lse_ref, block_ref, top_ref, total_ref, False
            )

        for k in range(copies):
            out_ref[k] = lse_ref[...]


def whole(array):
    zeros = (0,) * array.ndim
    return pl.BlockSpec(array.shape, lambda g, _: zeros, pipeline_mode=pl.Buffered(1))


def column_pass(picks, pieces, high, picks_t, exps, logits, copies):
    groups = exps.shape[0]
    rows = high.shape[0]
    return pl.pallas_call(
        functools.partial(column_kernel, copies),
        grid_spec=pltpu.PrefetchScalarGridSpec(
            num_scalar_prefetch=1,
            grid=(groups,),
            in_specs=[
                whole(pieces),
                whole(high),
                whole(picks_t),
                pl.BlockSpec((1, *exps.shape[1:]), lambda g, _: (g, 0, 0)),
                pl.BlockSpec(memory_space=pl.ANY),
            ],
            out_specs=[
                pl.BlockSpec((rows, BLK), lambda g, _: (0, 0)),
                pl.BlockSpec((copies, GB, BLK), lambda g, _: (0, 0, 0)),
            ],
            scratch_shapes=[
                pltpu.VMEM((rows, BLK), jnp.float32),
                pltpu.VMEM((rows, CAP * BLK), jnp.float32),
                pltpu.SMEM((1,), jnp.float32),
                pltpu.VMEM((GB, BLK), jnp.float32),
                pltpu.VMEM(exps.shape[1:], jnp.bfloat16),
                pltpu.VMEM((GB, BLK), jnp.float32),
                pltpu.VMEM((GB, BLK), jnp.float32),
            ],
        ),
        out_shape=[
            jax.ShapeDtypeStruct((rows, BLK), jnp.float32),
            jax.ShapeDtypeStruct((copies, GB, BLK), jnp.float32),
        ],
        compiler_params=pltpu.CompilerParams(vmem_limit_bytes=VMEM),
        name="column_pass",
    )(picks, pieces, high, picks_t, exps, logits)


def row_pass(picks, pieces, high, picks_v, exps, logits, copies, log_ratio):
    groups = exps.shape[0]
    rows = high.shape[0]
    return pl.pallas_call(
        functools.partial(row_kernel, copies, log_ratio),
        grid_spec=pltpu.PrefetchScalarGridSpec(
            num_scalar_prefetch=1,
            grid=(groups,),
            in_specs=[
                whole(pieces),
                whole(high),
                whole(picks_v),
                pl.BlockSpec((1, *exps.shape[1:]), lambda g, _: (g, 0, 0)),
                pl.BlockSpec(memory_space=pl.ANY),
            ],
            out_specs=pl.BlockSpec((copies, rows, BLK), lambda g, _: (0, 0, 0)),
            scratch_shapes=[
                pltpu.VMEM((GB, BLK), jnp.float32),
                pltpu.VMEM((rows, CAP * BLK), jnp.float32),
                pltpu.VMEM((rows, BLK), jnp.float32),
                pltpu.SMEM((1,), jnp.float32),
                pltpu.VMEM((rows, BLK), jnp.float32),
                pltpu.VMEM(exps.shape[1:], jnp.bfloat16),
                pltpu.VMEM((rows, BLK), jnp.float32),
                pltpu.VMEM((rows, BLK), jnp.float32),
            ],
        ),
        out_shape=jax.ShapeDtypeStruct((copies, rows, BLK), jnp.float32),
        compiler_params=pltpu.CompilerParams(vmem_limit_bytes=VMEM),
        name="row_pass",
    )(picks, pieces, high, picks_v, exps, logits)


def candidates(pattern, low_block):
    rows, slots = pattern.shape
    first = jnp.sum((pattern < low_block).astype(jnp.int32), axis=1)
    position = first[:, None] + jnp.arange(8, dtype=jnp.int32)[None, :]
    here = position[:, :, None] == jnp.arange(slots, dtype=jnp.int32)[None, None, :]
    offset = pattern - low_block
    found = jnp.max(jnp.where(here, offset[:, None, :], -1), axis=2)
    fits = (found < GB) & (jnp.arange(8, dtype=jnp.int32)[None, :] < CAP)
    return jnp.where(fits, found, -1)


def shards(frames, codes, pattern):
    gathered = lax.all_gather(frames, CODES, axis=0, tiled=True)
    feature_width = codes.shape[1]
    num_blocks = codes.shape[0] // BLK
    frame_count = pattern.shape[0]
    picked = candidates(pattern, lax.axis_index(CODES) * num_blocks)
    picks = picked.reshape(-1)
    frames_total = frame_count * BLK * lax.axis_size(FRAMES)
    codes_total = num_blocks * BLK * lax.axis_size(CODES)
    log_ratio = math.log(frames_total / codes_total)
    code_copies = lax.axis_size(CODES)
    frame_copies = lax.axis_size(FRAMES)
    exps, logits, high, lse = make_tiles(
        picks, gathered, codes.reshape(num_blocks, BLK, feature_width)
    )
    pieces = jnp.broadcast_to(lse[None], (code_copies, *lse.shape))
    for iteration in range(ITERS):
        pieces = lax.all_to_all(pieces, CODES, 0, 0, tiled=True)
        row_potential, pieces = column_pass(
            picks, pieces, high, picked.T, exps, logits, frame_copies
        )
        pieces = lax.all_to_all(pieces, FRAMES, 0, 0, tiled=True)
        if iteration < ITERS - 1:
            pieces = row_pass(
                picks, pieces, high, picked, exps, logits, code_copies, log_ratio
            )
    highest = jnp.max(pieces, axis=0)
    summed = jnp.sum(jnp.exp(pieces - highest[None]), axis=0)
    col_potential = log_ratio - (highest + jnp.log(summed))
    return (row_potential.reshape(-1), col_potential.reshape(-1))


def solution(mesh):
    torus = Mesh(mesh.devices.reshape(4, 8, 4, 2), ("frames_0", "frames_1", "codes_0", "codes_1"))
    placed = (P(FRAMES_CODES, None), P(CODES, None), P(FRAMES, None))
    return jax.shard_map(
        shards, mesh=torus, in_specs=placed, out_specs=(P(FRAMES), P(CODES)), check_vma=False
    )
```

```python
import functools
import math

import jax
import jax.numpy as jnp
from jax import lax
from jax.experimental import pallas as pl
from jax.experimental.pallas import tpu as pltpu
from jax.sharding import Mesh
from jax.sharding import PartitionSpec as P

BLK = 128
GB = 64
CAP = 6
ITERS = 3
PER = 8
CODES = ("codes_0", "codes_1")
FRAMES = ("frames_0", "frames_1")
FRAMES_CODES = ("frames_0", "frames_1", "codes_0", "codes_1")

NEG_FILL = -1e30
NEG_ROW = -1e29
SMALL = 1e-26
VMEM = 14 * 1024 * 1024


def tiles_kernel(picks, frames_ref, codes_ref, exp_ref, logit_ref, high_ref, lse_ref):
    group = pl.program_id(0)
    for b in range(PER):
        lanes = slice(b * BLK, (b + 1) * BLK)
        block = frames_ref[lanes, :] * jnp.bfloat16(2.0)
        top = None
        for s in range(CAP):
            pick = picks[(group * PER + b) * 8 + s]
            chosen = codes_ref[jnp.maximum(pick, 0)]
            tile = lax.dot_general(
                chosen, block, (((1,), (1,)), ((), ())), preferred_element_type=jnp.float32
            )
            tile = jnp.where(pick >= 0, tile, NEG_FILL).astype(jnp.bfloat16)
            logit_ref[0, s * BLK : (s + 1) * BLK, lanes] = tile
            part = jnp.max(tile.astype(jnp.float32).reshape(BLK // 8, 8, BLK), axis=0)
            top = part if top is None else jnp.maximum(top, part)
        high = jnp.maximum(jnp.max(top, axis=0, keepdims=True), NEG_ROW)
        total = None
        for s in range(CAP):
            tile = logit_ref[0, s * BLK : (s + 1) * BLK, lanes].astype(jnp.float32)
            terms = jnp.exp(tile - high)
            exp_ref[0, s * BLK : (s + 1) * BLK, lanes] = terms.astype(jnp.bfloat16)
            part = jnp.sum(terms.reshape(BLK // 8, 8, BLK), axis=0)
            total = part if total is None else total + part
        total = jnp.sum(total, axis=0, keepdims=True)
        high_ref[b : b + 1, :] = high
        lse_ref[b : b + 1, :] = jnp.where(total > 0.0, high + jnp.log(total), NEG_FILL)


def make_tiles(picks, frames, codes):
    groups = frames.shape[0] // (PER * BLK)
    rows = groups * PER
    return pl.pallas_call(
        tiles_kernel,
        grid_spec=pltpu.PrefetchScalarGridSpec(
            num_scalar_prefetch=1,
            grid=(groups,),
            in_specs=[
                pl.BlockSpec((PER * BLK, frames.shape[1]), lambda g, _: (g, 0)),
                pl.BlockSpec(codes.shape, lambda g, _: (0, 0, 0), pipeline_mode=pl.Buffered(1)),
            ],
            out_specs=[
                pl.BlockSpec((1, CAP * BLK, PER * BLK), lambda g, _: (g, 0, 0)),
                pl.BlockSpec((1, CAP * BLK, PER * BLK), lambda g, _: (g, 0, 0)),
                pl.BlockSpec((PER, BLK), lambda g, _: (g, 0)),
                pl.BlockSpec((PER, BLK), lambda g, _: (g, 0)),
            ],
        ),
        out_shape=[
            jax.ShapeDtypeStruct((groups, CAP * BLK, PER * BLK), jnp.bfloat16),
            jax.ShapeDtypeStruct((groups, CAP * BLK, PER * BLK), jnp.bfloat16),
            jax.ShapeDtypeStruct((rows, BLK), jnp.float32),
            jax.ShapeDtypeStruct((rows, BLK), jnp.float32),
        ],
        compiler_params=pltpu.CompilerParams(vmem_limit_bytes=VMEM),
        name="make_tiles",
    )(picks, frames, codes)


def log_sum(pieces_ref):
    count = pieces_ref.shape[0]
    high = pieces_ref[0]
    for k in range(1, count):
        high = jnp.maximum(high, pieces_ref[k])
    total = jnp.exp(pieces_ref[0] - high)
    for k in range(1, count):
        total = total + jnp.exp(pieces_ref[k] - high)
    return high + jnp.log(total)


def split_dot(selector, values):
    upper = values.astype(jnp.bfloat16)
    lower = (values - upper.astype(jnp.float32)).astype(jnp.bfloat16)
    return jnp.dot(selector, upper, preferred_element_type=jnp.float32) + jnp.dot(
        selector, lower, preferred_element_type=jnp.float32
    )


def stable_pass(picks, logit_ref, shift_ref, out_ref, block_ref, high_ref, total_ref, by_code):
    high_ref[...] = jnp.full_like(high_ref, NEG_FILL)
    total_ref[...] = jnp.zeros_like(total_ref)

    def one_group(g, _):
        pltpu.sync_copy(logit_ref.at[g], block_ref)

        def one_tile(index, _):
            b = index // CAP
            s = index - b * CAP
            row = g * PER + b
            pick = picks[row * 8 + s]

            @pl.when(pick >= 0)
            def _():
                rows = pl.ds(pl.multiple_of(s * BLK, BLK), BLK)
                lanes = pl.ds(pl.multiple_of(b * BLK, BLK), BLK)
                tile = block_ref[rows, lanes].astype(jnp.float32)
                if by_code:
                    tile = jnp.transpose(tile + shift_ref[pl.ds(row, 1), :])
                    at = pl.ds(pick, 1)
                else:
                    shift = jnp.broadcast_to(shift_ref[pl.ds(pick, 1), :], (BLK, BLK))
                    tile = tile + jnp.transpose(shift)
                    at = pl.ds(row, 1)
                before = high_ref[at, :]
                high = jnp.maximum(before, jnp.max(tile, axis=0, keepdims=True))
                total_ref[at, :] = total_ref[at, :] * jnp.exp(before - high) + jnp.sum(
                    jnp.exp(tile - high), axis=0, keepdims=True
                )
                high_ref[at, :] = high

            return 0

        lax.fori_loop(0, CAP * PER, one_tile, 0)
        return 0

    lax.fori_loop(0, logit_ref.shape[0], one_group, 0)
    total = total_ref[...]
    out_ref[...] = jnp.where(
        total > 0.0, high_ref[...] + jnp.log(jnp.maximum(total, 1e-37)), NEG_FILL
    )


def column_kernel(
    copies, picks, pieces_ref, high_ref, picks_ref, exp_ref, logit_ref, row_ref, out_ref,
    scale_ref, sums_ref, peak_ref, lse_ref, block_ref, top_ref, total_ref,
):
    group = pl.program_id(0)

    @pl.when(group == 0)
    def _():
        row = -log_sum(pieces_ref)
        row_ref[...] = row
        weight = high_ref[...] + row
        peak = jnp.max(weight)
        peak_ref[0] = peak
        scale_ref[...] = jnp.exp(weight - peak)

    scale = scale_ref[pl.ds(pl.multiple_of(group * PER, PER), PER), :]
    wide = jnp.concatenate([scale] * PER, axis=1)
    lane_block = lax.broadcasted_iota(jnp.int32, wide.shape, 1) // BLK
    row_block = lax.broadcasted_iota(jnp.int32, wide.shape, 0)
    wide = jnp.where(lane_block == row_block, wide, 0.0).astype(jnp.bfloat16)
    sums_ref[pl.ds(pl.multiple_of(group * PER, PER), PER), :] = lax.dot_general(
        wide, exp_ref[0], (((1,), (1,)), ((), ())), preferred_element_type=jnp.float32
    )

    @pl.when(group == pl.num_programs(0) - 1)
    def _():
        blocks = lax.broadcasted_iota(jnp.int32, (GB, picks_ref.shape[1]), 0)
        total = jnp.zeros(lse_ref.shape, jnp.float32)
        used = jnp.zeros((GB, 1), jnp.float32)
        for s in range(CAP):
            hit = (picks_ref[s : s + 1, :] == blocks).astype(jnp.float32)
            used = used + jnp.sum(hit, axis=1, keepdims=True)
            total = total + split_dot(
                hit.astype(jnp.bfloat16), sums_ref[:, s * BLK : (s + 1) * BLK]
            )
        lse_ref[...] = jnp.where(
            total > 0.0, peak_ref[0] + jnp.log(jnp.maximum(total, 1e-37)), NEG_FILL
        )
        low = jnp.min(jnp.where(used > 0.0, total, 1.0))

        @pl.when(jnp.logical_not(low >= SMALL))
        def _():
            stable_pass(
                picks, logit_ref, row_ref, lse_ref, block_ref, top_ref, total_ref, True
            )

        for k in range(copies):
            out_ref[k] = lse_ref[...]


def row_kernel(
    copies, log_ratio, picks, pieces_ref, high_ref, picks_ref, exp_ref, logit_ref, out_ref,
    col_ref, scale_ref, sums_ref, peak_ref, lse_ref, block_ref, top_ref, total_ref,
):
    group = pl.program_id(0)

    @pl.when(group == 0)
    def _():
        col = log_ratio - log_sum(pieces_ref)
        col_ref[...] = col
        peak = jnp.max(col)
        peak_ref[0] = peak
        scale = jnp.exp(col - peak).astype(jnp.bfloat16)
        blocks = lax.broadcasted_iota(jnp.int32, (picks_ref.shape[0], GB), 1)
        for s in range(CAP):
            hit = (picks_ref[:, s : s + 1] == blocks).astype(jnp.float32).astype(jnp.bfloat16)
            scale_ref[:, s * BLK : (s + 1) * BLK] = jnp.dot(
                hit, scale, preferred_element_type=jnp.float32
            )

    at = pl.ds(pl.multiple_of(group * PER, PER), PER)
    scale = scale_ref[at, :].astype(jnp.bfloat16)
    wide = jnp.dot(scale, exp_ref[0], preferred_element_type=jnp.float32)
    row_block = lax.broadcasted_iota(jnp.int32, (PER, BLK), 0)
    total = jnp.zeros((PER, BLK), jnp.float32)
    for b in range(PER):
        total = total + jnp.where(row_block == b, wide[:, b * BLK : (b + 1) * BLK], 0.0)
    sums_ref[at, :] = total

    @pl.when(group == pl.num_programs(0) - 1)
    def _():
        total = sums_ref[...]
        lse_ref[...] = jnp.where(
            total > 0.0,
            high_ref[...] + (peak_ref[0] + jnp.log(jnp.maximum(total, 1e-37))),
            NEG_FILL,
        )
        low = jnp.min(jnp.where(picks_ref[:, 0:1] >= 0, total, 1.0))

        @pl.when(jnp.logical_not(low >= SMALL))
        def _():
            stable_pass(
                picks, logit_ref, col_ref, lse_ref, block_ref, top_ref, total_ref, False
            )

        for k in range(copies):
            out_ref[k] = lse_ref[...]


def whole(array):
    zeros = (0,) * array.ndim
    return pl.BlockSpec(array.shape, lambda g, _: zeros, pipeline_mode=pl.Buffered(1))


def column_pass(picks, pieces, high, picks_t, exps, logits, copies):
    groups = exps.shape[0]
    rows = high.shape[0]
    return pl.pallas_call(
        functools.partial(column_kernel, copies),
        grid_spec=pltpu.PrefetchScalarGridSpec(
            num_scalar_prefetch=1,
            grid=(groups,),
            in_specs=[
                whole(pieces),
                whole(high),
                whole(picks_t),
                pl.BlockSpec((1, *exps.shape[1:]), lambda g, _: (g, 0, 0)),
                pl.BlockSpec(memory_space=pl.ANY),
            ],
            out_specs=[
                pl.BlockSpec((rows, BLK), lambda g, _: (0, 0)),
                pl.BlockSpec((copies, GB, BLK), lambda g, _: (0, 0, 0)),
            ],
            scratch_shapes=[
                pltpu.VMEM((rows, BLK), jnp.float32),
                pltpu.VMEM((rows, CAP * BLK), jnp.float32),
                pltpu.SMEM((1,), jnp.float32),
                pltpu.VMEM((GB, BLK), jnp.float32),
                pltpu.VMEM(exps.shape[1:], jnp.bfloat16),
                pltpu.VMEM((GB, BLK), jnp.float32),
                pltpu.VMEM((GB, BLK), jnp.float32),
            ],
        ),
        out_shape=[
            jax.ShapeDtypeStruct((rows, BLK), jnp.float32),
            jax.ShapeDtypeStruct((copies, GB, BLK), jnp.float32),
        ],
        compiler_params=pltpu.CompilerParams(vmem_limit_bytes=VMEM),
        name="column_pass",
    )(picks, pieces, high, picks_t, exps, logits)


def row_pass(picks, pieces, high, picks_v, exps, logits, copies, log_ratio):
    groups = exps.shape[0]
    rows = high.shape[0]
    return pl.pallas_call(
        functools.partial(row_kernel, copies, log_ratio),
        grid_spec=pltpu.PrefetchScalarGridSpec(
            num_scalar_prefetch=1,
            grid=(groups,),
            in_specs=[
                whole(pieces),
                whole(high),
                whole(picks_v),
                pl.BlockSpec((1, *exps.shape[1:]), lambda g, _: (g, 0, 0)),
                pl.BlockSpec(memory_space=pl.ANY),
            ],
            out_specs=pl.BlockSpec((copies, rows, BLK), lambda g, _: (0, 0, 0)),
            scratch_shapes=[
                pltpu.VMEM((GB, BLK), jnp.float32),
                pltpu.VMEM((rows, CAP * BLK), jnp.float32),
                pltpu.VMEM((rows, BLK), jnp.float32),
                pltpu.SMEM((1,), jnp.float32),
                pltpu.VMEM((rows, BLK), jnp.float32),
                pltpu.VMEM(exps.shape[1:], jnp.bfloat16),
                pltpu.VMEM((rows, BLK), jnp.float32),
                pltpu.VMEM((rows, BLK), jnp.float32),
            ],
        ),
        out_shape=jax.ShapeDtypeStruct((copies, rows, BLK), jnp.float32),
        compiler_params=pltpu.CompilerParams(vmem_limit_bytes=VMEM),
        name="row_pass",
    )(picks, pieces, high, picks_v, exps, logits)


def candidates(pattern, low_block):
    rows, slots = pattern.shape
    first = jnp.sum((pattern < low_block).astype(jnp.int32), axis=1)
    position = first[:, None] + jnp.arange(8, dtype=jnp.int32)[None, :]
    here = position[:, :, None] == jnp.arange(slots, dtype=jnp.int32)[None, None, :]
    offset = pattern - low_block
    found = jnp.max(jnp.where(here, offset[:, None, :], -1), axis=2)
    fits = (found < GB) & (jnp.arange(8, dtype=jnp.int32)[None, :] < CAP)
    return jnp.where(fits, found, -1)


def shards(frames, codes, pattern):
    gathered = lax.all_gather(frames, CODES, axis=0, tiled=True)
    feature_width = codes.shape[1]
    num_blocks = codes.shape[0] // BLK
    frame_count = pattern.shape[0]
    picked = candidates(pattern, lax.axis_index(CODES) * num_blocks)
    picks, picked, picked_t, gathered = lax.optimization_barrier(
        (picked.reshape(-1), picked, picked.T, gathered)
    )
    frames_total = frame_count * BLK * lax.axis_size(FRAMES)
    codes_total = num_blocks * BLK * lax.axis_size(CODES)
    log_ratio = math.log(frames_total / codes_total)
    code_copies = lax.axis_size(CODES)
    frame_copies = lax.axis_size(FRAMES)
    exps, logits, high, lse = make_tiles(
        picks, gathered, codes.reshape(num_blocks, BLK, feature_width)
    )
    pieces = jnp.broadcast_to(lse[None], (code_copies, *lse.shape))
    for iteration in range(ITERS):
        pieces = lax.all_to_all(pieces, CODES, 0, 0, tiled=True)
        row_potential, pieces = column_pass(
            picks, pieces, high, picked_t, exps, logits, frame_copies
        )
        pieces = lax.all_to_all(pieces, FRAMES, 0, 0, tiled=True)
        if iteration < ITERS - 1:
            pieces = row_pass(
                picks, pieces, high, picked, exps, logits, code_copies, log_ratio
            )
    highest = jnp.max(pieces, axis=0)
    summed = jnp.sum(jnp.exp(pieces - highest[None]), axis=0)
    col_potential = log_ratio - (highest + jnp.log(summed))
    return (row_potential.reshape(-1), col_potential.reshape(-1))


def solution(mesh):
    torus = Mesh(mesh.devices.reshape(4, 8, 4, 2), ("frames_0", "frames_1", "codes_0", "codes_1"))
    placed = (P(FRAMES_CODES, None), P(CODES, None), P(FRAMES, None))
    return jax.shard_map(
        shards, mesh=torus, in_specs=placed, out_specs=(P(FRAMES), P(CODES)), check_vma=False
    )
```

```python
import functools
import math

import jax
import jax.numpy as jnp
from jax import lax
from jax.experimental import pallas as pl
from jax.experimental.pallas import tpu as pltpu
from jax.sharding import Mesh
from jax.sharding import PartitionSpec as P

BLK = 128
GB = 64
CAP = 6
ITERS = 3
PER = 8
CODES = ("codes_0", "codes_1")
FRAMES = ("frames_0", "frames_1")
FRAMES_CODES = ("frames_0", "frames_1", "codes_0", "codes_1")

NEG_FILL = -1e30
NEG_ROW = -1e29
SMALL = 1e-26
VMEM = 14 * 1024 * 1024


def tiles_kernel(picks, chunk, frames_ref, codes_ref, *refs):
    exp_ref, logit_ref, high_ref, lse_ref = refs[-4:]
    for b in range(PER):
        lanes = slice(b * BLK, (b + 1) * BLK)
        block = frames_ref[lanes, :] * jnp.bfloat16(2.0)
        top = None
        for s in range(CAP):
            pick = picks[(chunk[0] * PER + b) * 8 + s]
            chosen = codes_ref[jnp.maximum(pick, 0)]
            tile = lax.dot_general(
                chosen, block, (((1,), (1,)), ((), ())), preferred_element_type=jnp.float32
            )
            tile = jnp.where(pick >= 0, tile, NEG_FILL).astype(jnp.bfloat16)
            logit_ref[0, s * BLK : (s + 1) * BLK, lanes] = tile
            part = jnp.max(tile.astype(jnp.float32).reshape(BLK // 8, 8, BLK), axis=0)
            top = part if top is None else jnp.maximum(top, part)
        high = jnp.maximum(jnp.max(top, axis=0, keepdims=True), NEG_ROW)
        total = None
        for s in range(CAP):
            tile = logit_ref[0, s * BLK : (s + 1) * BLK, lanes].astype(jnp.float32)
            terms = jnp.exp(tile - high)
            exp_ref[0, s * BLK : (s + 1) * BLK, lanes] = terms.astype(jnp.bfloat16)
            part = jnp.sum(terms.reshape(BLK // 8, 8, BLK), axis=0)
            total = part if total is None else total + part
        total = jnp.sum(total, axis=0, keepdims=True)
        high_ref[b : b + 1, :] = high
        lse_ref[b : b + 1, :] = jnp.where(total > 0.0, high + jnp.log(total), NEG_FILL)


def make_tiles(picks, chunk, frames, codes, chunks, before):
    tile_rows, tile_lanes = CAP * BLK, PER * BLK
    return pl.pallas_call(
        tiles_kernel,
        grid_spec=pltpu.PrefetchScalarGridSpec(
            num_scalar_prefetch=2,
            grid=(1,),
            in_specs=[
                pl.BlockSpec(frames.shape, lambda g, *_: (0, 0), pipeline_mode=pl.Buffered(1)),
                pl.BlockSpec(codes.shape, lambda g, *_: (0, 0, 0), pipeline_mode=pl.Buffered(1)),
                *[pl.BlockSpec(memory_space=pl.ANY) for _ in before],
            ],
            out_specs=[
                pl.BlockSpec((1, tile_rows, tile_lanes), lambda g, _, chunk: (chunk[0], 0, 0)),
                pl.BlockSpec((1, tile_rows, tile_lanes), lambda g, _, chunk: (chunk[0], 0, 0)),
                pl.BlockSpec((PER, BLK), lambda g, _, chunk: (chunk[0], 0)),
                pl.BlockSpec((PER, BLK), lambda g, _, chunk: (chunk[0], 0)),
            ],
        ),
        out_shape=[
            jax.ShapeDtypeStruct((chunks, tile_rows, tile_lanes), jnp.bfloat16),
            jax.ShapeDtypeStruct((chunks, tile_rows, tile_lanes), jnp.bfloat16),
            jax.ShapeDtypeStruct((chunks * PER, BLK), jnp.float32),
            jax.ShapeDtypeStruct((chunks * PER, BLK), jnp.float32),
        ],
        input_output_aliases={4 + k: k for k in range(len(before))},
        cost_estimate=pl.CostEstimate(
            flops=2 * tile_rows * tile_lanes * frames.shape[1],
            bytes_accessed=4 * tile_rows * tile_lanes,
            transcendentals=tile_rows * tile_lanes,
        ),
        compiler_params=pltpu.CompilerParams(vmem_limit_bytes=VMEM),
        name="make_tiles",
    )(picks, chunk, frames, codes, *before)


def log_sum(pieces_ref):
    count = pieces_ref.shape[0]
    high = pieces_ref[0]
    for k in range(1, count):
        high = jnp.maximum(high, pieces_ref[k])
    total = jnp.exp(pieces_ref[0] - high)
    for k in range(1, count):
        total = total + jnp.exp(pieces_ref[k] - high)
    return high + jnp.log(total)


def split_dot(selector, values):
    upper = values.astype(jnp.bfloat16)
    lower = (values - upper.astype(jnp.float32)).astype(jnp.bfloat16)
    return jnp.dot(selector, upper, preferred_element_type=jnp.float32) + jnp.dot(
        selector, lower, preferred_element_type=jnp.float32
    )


def stable_pass(picks, logit_ref, shift_ref, out_ref, block_ref, high_ref, total_ref, by_code):
    high_ref[...] = jnp.full_like(high_ref, NEG_FILL)
    total_ref[...] = jnp.zeros_like(total_ref)

    def one_group(g, _):
        pltpu.sync_copy(logit_ref.at[g], block_ref)

        def one_tile(index, _):
            b = index // CAP
            s = index - b * CAP
            row = g * PER + b
            pick = picks[row * 8 + s]

            @pl.when(pick >= 0)
            def _():
                rows = pl.ds(pl.multiple_of(s * BLK, BLK), BLK)
                lanes = pl.ds(pl.multiple_of(b * BLK, BLK), BLK)
                tile = block_ref[rows, lanes].astype(jnp.float32)
                if by_code:
                    tile = jnp.transpose(tile + shift_ref[pl.ds(row, 1), :])
                    at = pl.ds(pick, 1)
                else:
                    shift = jnp.broadcast_to(shift_ref[pl.ds(pick, 1), :], (BLK, BLK))
                    tile = tile + jnp.transpose(shift)
                    at = pl.ds(row, 1)
                before = high_ref[at, :]
                high = jnp.maximum(before, jnp.max(tile, axis=0, keepdims=True))
                total_ref[at, :] = total_ref[at, :] * jnp.exp(before - high) + jnp.sum(
                    jnp.exp(tile - high), axis=0, keepdims=True
                )
                high_ref[at, :] = high

            return 0

        lax.fori_loop(0, CAP * PER, one_tile, 0)
        return 0

    lax.fori_loop(0, logit_ref.shape[0], one_group, 0)
    total = total_ref[...]
    out_ref[...] = jnp.where(
        total > 0.0, high_ref[...] + jnp.log(jnp.maximum(total, 1e-37)), NEG_FILL
    )


def column_kernel(
    copies, picks, pieces_ref, high_ref, picks_ref, exp_ref, logit_ref, row_ref, out_ref,
    scale_ref, sums_ref, peak_ref, lse_ref, block_ref, top_ref, total_ref,
):
    group = pl.program_id(0)

    @pl.when(group == 0)
    def _():
        row = -log_sum(pieces_ref)
        row_ref[...] = row
        weight = high_ref[...] + row
        peak = jnp.max(weight)
        peak_ref[0] = peak
        scale_ref[...] = jnp.exp(weight - peak)

    scale = scale_ref[pl.ds(pl.multiple_of(group * PER, PER), PER), :]
    wide = jnp.concatenate([scale] * PER, axis=1)
    lane_block = lax.broadcasted_iota(jnp.int32, wide.shape, 1) // BLK
    row_block = lax.broadcasted_iota(jnp.int32, wide.shape, 0)
    wide = jnp.where(lane_block == row_block, wide, 0.0).astype(jnp.bfloat16)
    sums_ref[pl.ds(pl.multiple_of(group * PER, PER), PER), :] = lax.dot_general(
        wide, exp_ref[0], (((1,), (1,)), ((), ())), preferred_element_type=jnp.float32
    )

    @pl.when(group == pl.num_programs(0) - 1)
    def _():
        blocks = lax.broadcasted_iota(jnp.int32, (GB, picks_ref.shape[1]), 0)
        total = jnp.zeros(lse_ref.shape, jnp.float32)
        used = jnp.zeros((GB, 1), jnp.float32)
        for s in range(CAP):
            hit = (picks_ref[s : s + 1, :] == blocks).astype(jnp.float32)
            used = used + jnp.sum(hit, axis=1, keepdims=True)
            total = total + split_dot(
                hit.astype(jnp.bfloat16), sums_ref[:, s * BLK : (s + 1) * BLK]
            )
        lse_ref[...] = jnp.where(
            total > 0.0, peak_ref[0] + jnp.log(jnp.maximum(total, 1e-37)), NEG_FILL
        )
        low = jnp.min(jnp.where(used > 0.0, total, 1.0))

        @pl.when(jnp.logical_not(low >= SMALL))
        def _():
            stable_pass(
                picks, logit_ref, row_ref, lse_ref, block_ref, top_ref, total_ref, True
            )

        for k in range(copies):
            out_ref[k] = lse_ref[...]


def row_kernel(
    copies, log_ratio, picks, pieces_ref, high_ref, picks_ref, exp_ref, logit_ref, out_ref,
    col_ref, scale_ref, sums_ref, peak_ref, lse_ref, block_ref, top_ref, total_ref,
):
    group = pl.program_id(0)

    @pl.when(group == 0)
    def _():
        col = log_ratio - log_sum(pieces_ref)
        col_ref[...] = col
        peak = jnp.max(col)
        peak_ref[0] = peak
        scale = jnp.exp(col - peak).astype(jnp.bfloat16)
        blocks = lax.broadcasted_iota(jnp.int32, (picks_ref.shape[0], GB), 1)
        for s in range(CAP):
            hit = (picks_ref[:, s : s + 1] == blocks).astype(jnp.float32).astype(jnp.bfloat16)
            scale_ref[:, s * BLK : (s + 1) * BLK] = jnp.dot(
                hit, scale, preferred_element_type=jnp.float32
            )

    at = pl.ds(pl.multiple_of(group * PER, PER), PER)
    scale = scale_ref[at, :].astype(jnp.bfloat16)
    wide = jnp.dot(scale, exp_ref[0], preferred_element_type=jnp.float32)
    row_block = lax.broadcasted_iota(jnp.int32, (PER, BLK), 0)
    total = jnp.zeros((PER, BLK), jnp.float32)
    for b in range(PER):
        total = total + jnp.where(row_block == b, wide[:, b * BLK : (b + 1) * BLK], 0.0)
    sums_ref[at, :] = total

    @pl.when(group == pl.num_programs(0) - 1)
    def _():
        total = sums_ref[...]
        lse_ref[...] = jnp.where(
            total > 0.0,
            high_ref[...] + (peak_ref[0] + jnp.log(jnp.maximum(total, 1e-37))),
            NEG_FILL,
        )
        low = jnp.min(jnp.where(picks_ref[:, 0:1] >= 0, total, 1.0))

        @pl.when(jnp.logical_not(low >= SMALL))
        def _():
            stable_pass(
                picks, logit_ref, col_ref, lse_ref, block_ref, top_ref, total_ref, False
            )

        for k in range(copies):
            out_ref[k] = lse_ref[...]


def whole(array):
    zeros = (0,) * array.ndim
    return pl.BlockSpec(array.shape, lambda g, _: zeros, pipeline_mode=pl.Buffered(1))


def column_pass(picks, pieces, high, picks_t, exps, logits, copies):
    groups = exps.shape[0]
    rows = high.shape[0]
    return pl.pallas_call(
        functools.partial(column_kernel, copies),
        grid_spec=pltpu.PrefetchScalarGridSpec(
            num_scalar_prefetch=1,
            grid=(groups,),
            in_specs=[
                whole(pieces),
                whole(high),
                whole(picks_t),
                pl.BlockSpec((1, *exps.shape[1:]), lambda g, _: (g, 0, 0)),
                pl.BlockSpec(memory_space=pl.ANY),
            ],
            out_specs=[
                pl.BlockSpec((rows, BLK), lambda g, _: (0, 0)),
                pl.BlockSpec((copies, GB, BLK), lambda g, _: (0, 0, 0)),
            ],
            scratch_shapes=[
                pltpu.VMEM((rows, BLK), jnp.float32),
                pltpu.VMEM((rows, CAP * BLK), jnp.float32),
                pltpu.SMEM((1,), jnp.float32),
                pltpu.VMEM((GB, BLK), jnp.float32),
                pltpu.VMEM(exps.shape[1:], jnp.bfloat16),
                pltpu.VMEM((GB, BLK), jnp.float32),
                pltpu.VMEM((GB, BLK), jnp.float32),
            ],
        ),
        out_shape=[
            jax.ShapeDtypeStruct((rows, BLK), jnp.float32),
            jax.ShapeDtypeStruct((copies, GB, BLK), jnp.float32),
        ],
        compiler_params=pltpu.CompilerParams(vmem_limit_bytes=VMEM),
        name="column_pass",
    )(picks, pieces, high, picks_t, exps, logits)


def row_pass(picks, pieces, high, picks_v, exps, logits, copies, log_ratio):
    groups = exps.shape[0]
    rows = high.shape[0]
    return pl.pallas_call(
        functools.partial(row_kernel, copies, log_ratio),
        grid_spec=pltpu.PrefetchScalarGridSpec(
            num_scalar_prefetch=1,
            grid=(groups,),
            in_specs=[
                whole(pieces),
                whole(high),
                whole(picks_v),
                pl.BlockSpec((1, *exps.shape[1:]), lambda g, _: (g, 0, 0)),
                pl.BlockSpec(memory_space=pl.ANY),
            ],
            out_specs=pl.BlockSpec((copies, rows, BLK), lambda g, _: (0, 0, 0)),
            scratch_shapes=[
                pltpu.VMEM((GB, BLK), jnp.float32),
                pltpu.VMEM((rows, CAP * BLK), jnp.float32),
                pltpu.VMEM((rows, BLK), jnp.float32),
                pltpu.SMEM((1,), jnp.float32),
                pltpu.VMEM((rows, BLK), jnp.float32),
                pltpu.VMEM(exps.shape[1:], jnp.bfloat16),
                pltpu.VMEM((rows, BLK), jnp.float32),
                pltpu.VMEM((rows, BLK), jnp.float32),
            ],
        ),
        out_shape=jax.ShapeDtypeStruct((copies, rows, BLK), jnp.float32),
        compiler_params=pltpu.CompilerParams(vmem_limit_bytes=VMEM),
        name="row_pass",
    )(picks, pieces, high, picks_v, exps, logits)


def candidates(pattern, low_block):
    rows, slots = pattern.shape
    first = jnp.sum((pattern < low_block).astype(jnp.int32), axis=1)
    position = first[:, None] + jnp.arange(8, dtype=jnp.int32)[None, :]
    here = position[:, :, None] == jnp.arange(slots, dtype=jnp.int32)[None, None, :]
    offset = pattern - low_block
    found = jnp.max(jnp.where(here, offset[:, None, :], -1), axis=2)
    fits = (found < GB) & (jnp.arange(8, dtype=jnp.int32)[None, :] < CAP)
    return jnp.where(fits, found, -1)


def ring_shift(array, axis, step):
    size = lax.axis_size(axis)
    return lax.ppermute(array, axis, [(k, (k + step) % size) for k in range(size)])


def combine_kernel(offset, sign, pieces_ref, out_ref):
    lse = pieces_ref[0] if pieces_ref.shape[0] == 1 else log_sum(pieces_ref)
    lse = offset + sign * lse
    for k in range(out_ref.shape[0]):
        out_ref[k] = lse


def combine(pieces, copies, offset=0.0, sign=1.0):
    return pl.pallas_call(
        functools.partial(combine_kernel, offset, sign),
        out_shape=jax.ShapeDtypeStruct((copies, *pieces.shape[1:]), jnp.float32),
        compiler_params=pltpu.CompilerParams(vmem_limit_bytes=VMEM),
        name="combine",
    )(pieces)


def shards(frames, codes, pattern):
    along, core = CODES
    chips, cores = lax.axis_size(along), lax.axis_size(core)
    chip, half = lax.axis_index(along), lax.axis_index(core)
    code_copies = chips * cores
    steps = ((0,), (1, chips - 1), (2,))
    came = {k: ring_shift(frames, along, k) if k else frames for step in steps for k in step}
    feature_width = codes.shape[1]
    num_blocks = codes.shape[0] // BLK
    frame_count = pattern.shape[0]
    picked = candidates(pattern, lax.axis_index(CODES) * num_blocks)
    codes = codes.reshape(num_blocks, BLK, feature_width)
    places = {
        (k, mine): (((chip - k) % chips) * cores + (half + mine) % cores).reshape(1)
        for step in steps
        for k in step
        for mine in (0, 1)
    }
    picks, picked, picked_t, codes, places = lax.optimization_barrier(
        (picked.reshape(-1), picked, picked.T, codes, places)
    )
    frames_total = frame_count * BLK * lax.axis_size(FRAMES)
    codes_total = num_blocks * BLK * lax.axis_size(CODES)
    log_ratio = math.log(frames_total / codes_total)
    made = ()
    for step in steps:
        blocks, made = lax.optimization_barrier((tuple(came[k] for k in step), made))
        other = tuple(ring_shift(block, core, 1) for block in blocks)
        for mine, group in enumerate((blocks, other)):
            for k, block in zip(step, group):
                made = make_tiles(picks, places[k, mine], block, codes, code_copies, made)
    exps, logits, high, lse = made
    first, second = FRAMES
    pieces = combine(lse[None], code_copies)
    for iteration in range(ITERS):
        pieces = lax.all_to_all(pieces, CODES, 0, 0, tiled=True)
        row_potential, pieces = column_pass(
            picks, pieces, high, picked_t, exps, logits, lax.axis_size(first)
        )
        pieces = lax.all_to_all(pieces, first, 0, 0, tiled=True)
        pieces = combine(pieces, lax.axis_size(second))
        pieces = lax.all_to_all(pieces, second, 0, 0, tiled=True)
        if iteration < ITERS - 1:
            pieces = row_pass(
                picks, pieces, high, picked, exps, logits, code_copies, log_ratio
            )
    col_potential = combine(pieces, 1, log_ratio, -1.0)
    return (row_potential.reshape(-1), col_potential.reshape(-1))


def solution(mesh):
    torus = Mesh(mesh.devices.reshape(4, 8, 4, 2), ("frames_0", "frames_1", "codes_0", "codes_1"))
    placed = (P(FRAMES_CODES, None), P(CODES, None), P(FRAMES, None))
    return jax.shard_map(
        shards, mesh=torus, in_specs=placed, out_specs=(P(FRAMES), P(CODES)), check_vma=False
    )
```

```python
import functools
import math

import jax
import jax.numpy as jnp
from jax import lax
from jax.experimental import pallas as pl
from jax.experimental.pallas import tpu as pltpu
from jax.sharding import Mesh
from jax.sharding import PartitionSpec as P


BLK = 128
GB = 64
CAP = 6
ITERS = 3
PER = 8
CODES = ("codes_0", "codes_1")
FRAMES = ("frames_0", "frames_1")
FRAMES_CODES = ("frames_0", "frames_1", "codes_0", "codes_1")

NEG_FILL = -1e30
NEG_ROW = -1e29
SMALL = 1e-26
VMEM = 14 * 1024 * 1024


def tiles_kernel(picks, chunk, frames_ref, codes_ref, *refs):
    exp_ref, logit_ref, high_ref, lse_ref = refs[-4:]
    for b in range(PER):
        block = frames_ref[b * BLK : (b + 1) * BLK, :] * jnp.bfloat16(2.0)
        first = picks[(chunk[0] * PER + b) * 8]
        filled = []
        top = None
        for s in range(CAP):
            pick = picks[(chunk[0] * PER + b) * 8 + s]
            chosen = codes_ref[jnp.maximum(jnp.where(pick >= 0, pick, first), 0)]
            filled.append(jnp.where(pick >= 0, 1.0, 0.0))
            tile = lax.dot_general(
                chosen, block, (((1,), (1,)), ((), ())), preferred_element_type=jnp.float32
            )
            logit_ref[b, s * BLK : (s + 1) * BLK, :] = tile.astype(jnp.bfloat16)
            part = jnp.max(tile.reshape(BLK // 8, 8, BLK), axis=0)
            top = part if top is None else jnp.maximum(top, part)
        high = jnp.max(top, axis=0, keepdims=True).astype(jnp.bfloat16).astype(jnp.float32)
        total = None
        for s in range(CAP):
            tile = logit_ref[b, s * BLK : (s + 1) * BLK, :].astype(jnp.float32)
            terms = jnp.exp(tile - high)
            exp_ref[b, s * BLK : (s + 1) * BLK, :] = terms.astype(jnp.bfloat16)
            part = jnp.sum(terms.reshape(BLK // 8, 8, BLK), axis=0) * filled[s]
            total = part if total is None else total + part
        total = jnp.sum(total, axis=0, keepdims=True)
        high_ref[b : b + 1, :] = jnp.where(first >= 0, high, NEG_ROW)
        lse_ref[b : b + 1, :] = jnp.where(first >= 0, high + jnp.log(total), NEG_FILL)


def make_tiles(picks, chunk, frames, codes, chunks, before):
    tile_rows = CAP * BLK
    tiles = pl.BlockSpec((PER, tile_rows, BLK), lambda g, _, chunk: (chunk[0], 0, 0))
    lines = pl.BlockSpec((PER, BLK), lambda g, _, chunk: (chunk[0], 0))
    tiles_shape = jax.ShapeDtypeStruct((chunks * PER, tile_rows, BLK), jnp.bfloat16)
    lines_shape = jax.ShapeDtypeStruct((chunks * PER, BLK), jnp.float32)
    return pl.pallas_call(
        tiles_kernel,
        grid_spec=pltpu.PrefetchScalarGridSpec(
            num_scalar_prefetch=2,
            grid=(1,),
            in_specs=[
                pl.BlockSpec(frames.shape, lambda g, *_: (0, 0), pipeline_mode=pl.Buffered(1)),
                pl.BlockSpec(codes.shape, lambda g, *_: (0, 0, 0), pipeline_mode=pl.Buffered(1)),
                *[pl.BlockSpec(memory_space=pl.ANY) for _ in before],
            ],
            out_specs=[tiles, tiles, lines, lines],
        ),
        out_shape=[tiles_shape, tiles_shape, lines_shape, lines_shape],
        input_output_aliases={4 + k: k for k in range(len(before))},
        cost_estimate=pl.CostEstimate(
            flops=2 * tile_rows * PER * BLK * frames.shape[1],
            bytes_accessed=4 * tile_rows * PER * BLK,
            transcendentals=tile_rows * PER * BLK,
        ),
        compiler_params=pltpu.CompilerParams(vmem_limit_bytes=VMEM),
        name="make_tiles",
    )(picks, chunk, frames, codes, *before)


def pair(tiles_ref, q):
    return jnp.concatenate([tiles_ref[2 * q], tiles_ref[2 * q + 1]], axis=1)


def log_sum(pieces_ref):
    count = pieces_ref.shape[0]
    high = pieces_ref[0]
    for k in range(1, count):
        high = jnp.maximum(high, pieces_ref[k])
    total = jnp.exp(pieces_ref[0] - high)
    for k in range(1, count):
        total = total + jnp.exp(pieces_ref[k] - high)
    return high + jnp.log(total)


def split_dot(selector, values):
    upper = values.astype(jnp.bfloat16)
    lower = (values - upper.astype(jnp.float32)).astype(jnp.bfloat16)
    return jnp.dot(selector, upper, preferred_element_type=jnp.float32) + jnp.dot(
        selector, lower, preferred_element_type=jnp.float32
    )


def stable_pass(picks, logit_ref, shift_ref, out_ref, block_ref, high_ref, total_ref, by_code):
    high_ref[...] = jnp.full_like(high_ref, NEG_FILL)
    total_ref[...] = jnp.zeros_like(total_ref)

    def one_group(g, _):
        pltpu.sync_copy(logit_ref.at[pl.ds(g * PER, PER)], block_ref)

        def one_tile(index, _):
            b = index // CAP
            s = index - b * CAP
            row = g * PER + b
            pick = picks[row * 8 + s]

            @pl.when(pick >= 0)
            def _():
                rows = pl.ds(pl.multiple_of(s * BLK, BLK), BLK)
                tile = block_ref[b, rows, :].astype(jnp.float32)
                if by_code:
                    tile = jnp.transpose(tile + shift_ref[pl.ds(row, 1), :])
                    at = pl.ds(pick, 1)
                else:
                    shift = jnp.broadcast_to(shift_ref[pl.ds(pick, 1), :], (BLK, BLK))
                    tile = tile + jnp.transpose(shift)
                    at = pl.ds(row, 1)
                before = high_ref[at, :]
                high = jnp.maximum(before, jnp.max(tile, axis=0, keepdims=True))
                total_ref[at, :] = total_ref[at, :] * jnp.exp(before - high) + jnp.sum(
                    jnp.exp(tile - high), axis=0, keepdims=True
                )
                high_ref[at, :] = high

            return 0

        lax.fori_loop(0, CAP * PER, one_tile, 0)
        return 0

    lax.fori_loop(0, logit_ref.shape[0] // PER, one_group, 0)
    total = total_ref[...]
    out_ref[...] = jnp.where(
        total > 0.0, high_ref[...] + jnp.log(jnp.maximum(total, 1e-37)), NEG_FILL
    )


def column_kernel(
    copies, picks, pieces_ref, high_ref, picks_ref, exp_ref, logit_ref, row_ref, out_ref,
    scale_ref, sums_ref, peak_ref, lse_ref, block_ref, top_ref, total_ref,
):
    group = pl.program_id(0)

    @pl.when(group == 0)
    def _():
        row = -log_sum(pieces_ref)
        row_ref[...] = row
        weight = high_ref[...] + row
        peak = jnp.max(weight)
        peak_ref[0] = peak
        scale_ref[...] = jnp.exp(weight - peak)

    scale = scale_ref[pl.ds(pl.multiple_of(group * PER, PER), PER), :]
    wide = jnp.concatenate([scale] * PER, axis=1)
    lane_block = lax.broadcasted_iota(jnp.int32, wide.shape, 1) // BLK
    row_block = lax.broadcasted_iota(jnp.int32, wide.shape, 0)
    wide = jnp.where(lane_block == row_block, wide, 0.0).astype(jnp.bfloat16)
    sums = None
    for q in range(PER // 2):
        part = lax.dot_general(
            wide[:, 2 * q * BLK : 2 * (q + 1) * BLK],
            pair(exp_ref, q),
            (((1,), (1,)), ((), ())),
            preferred_element_type=jnp.float32,
        )
        sums = part if sums is None else sums + part
    sums_ref[pl.ds(pl.multiple_of(group * PER, PER), PER), :] = sums

    @pl.when(group == pl.num_programs(0) - 1)
    def _():
        blocks = lax.broadcasted_iota(jnp.int32, (GB, picks_ref.shape[1]), 0)
        total = jnp.zeros(lse_ref.shape, jnp.float32)
        used = jnp.zeros((GB, 1), jnp.float32)
        for s in range(CAP):
            hit = (picks_ref[s : s + 1, :] == blocks).astype(jnp.float32)
            used = used + jnp.sum(hit, axis=1, keepdims=True)
            total = total + split_dot(
                hit.astype(jnp.bfloat16), sums_ref[:, s * BLK : (s + 1) * BLK]
            )
        lse_ref[...] = jnp.where(
            total > 0.0, peak_ref[0] + jnp.log(jnp.maximum(total, 1e-37)), NEG_FILL
        )
        low = jnp.min(jnp.where(used > 0.0, total, 1.0))

        @pl.when(jnp.logical_not(low >= SMALL))
        def _():
            stable_pass(
                picks, logit_ref, row_ref, lse_ref, block_ref, top_ref, total_ref, True
            )

        for k in range(copies):
            out_ref[k] = lse_ref[...]


def row_kernel(
    copies, log_ratio, picks, pieces_ref, high_ref, picks_ref, exp_ref, logit_ref, out_ref,
    col_ref, scale_ref, sums_ref, peak_ref, lse_ref, block_ref, top_ref, total_ref,
):
    group = pl.program_id(0)

    @pl.when(group == 0)
    def _():
        col = log_ratio - log_sum(pieces_ref)
        col_ref[...] = col
        peak = jnp.max(col)
        peak_ref[0] = peak
        scale = jnp.exp(col - peak).astype(jnp.bfloat16)
        blocks = lax.broadcasted_iota(jnp.int32, (picks_ref.shape[0], GB), 1)
        for s in range(CAP):
            hit = (picks_ref[:, s : s + 1] == blocks).astype(jnp.float32).astype(jnp.bfloat16)
            scale_ref[:, s * BLK : (s + 1) * BLK] = jnp.dot(
                hit, scale, preferred_element_type=jnp.float32
            )

    at = pl.ds(pl.multiple_of(group * PER, PER), PER)
    scale = scale_ref[at, :].astype(jnp.bfloat16)
    row_block = lax.broadcasted_iota(jnp.int32, (PER, BLK), 0)
    total = jnp.zeros((PER, BLK), jnp.float32)
    for q in range(PER // 2):
        wide = jnp.dot(scale, pair(exp_ref, q), preferred_element_type=jnp.float32)
        total = total + jnp.where(row_block == 2 * q, wide[:, :BLK], 0.0)
        total = total + jnp.where(row_block == 2 * q + 1, wide[:, BLK:], 0.0)
    sums_ref[at, :] = total

    @pl.when(group == pl.num_programs(0) - 1)
    def _():
        total = sums_ref[...]
        lse_ref[...] = jnp.where(
            total > 0.0,
            high_ref[...] + (peak_ref[0] + jnp.log(jnp.maximum(total, 1e-37))),
            NEG_FILL,
        )
        low = jnp.min(jnp.where(picks_ref[:, 0:1] >= 0, total, 1.0))

        @pl.when(jnp.logical_not(low >= SMALL))
        def _():
            stable_pass(
                picks, logit_ref, col_ref, lse_ref, block_ref, top_ref, total_ref, False
            )

        for k in range(copies):
            out_ref[k] = lse_ref[...]


def whole(array):
    zeros = (0,) * array.ndim
    return pl.BlockSpec(array.shape, lambda g, _: zeros, pipeline_mode=pl.Buffered(1))


def column_pass(picks, pieces, high, picks_t, exps, logits, copies):
    groups = exps.shape[0] // PER
    rows = high.shape[0]
    return pl.pallas_call(
        functools.partial(column_kernel, copies),
        grid_spec=pltpu.PrefetchScalarGridSpec(
            num_scalar_prefetch=1,
            grid=(groups,),
            in_specs=[
                whole(pieces),
                whole(high),
                whole(picks_t),
                pl.BlockSpec((PER, *exps.shape[1:]), lambda g, _: (g, 0, 0)),
                pl.BlockSpec(memory_space=pl.ANY),
            ],
            out_specs=[
                pl.BlockSpec((rows, BLK), lambda g, _: (0, 0)),
                pl.BlockSpec((copies, GB, BLK), lambda g, _: (0, 0, 0)),
            ],
            scratch_shapes=[
                pltpu.VMEM((rows, BLK), jnp.float32),
                pltpu.VMEM((rows, CAP * BLK), jnp.float32),
                pltpu.SMEM((1,), jnp.float32),
                pltpu.VMEM((GB, BLK), jnp.float32),
                pltpu.VMEM((PER, *exps.shape[1:]), jnp.bfloat16),
                pltpu.VMEM((GB, BLK), jnp.float32),
                pltpu.VMEM((GB, BLK), jnp.float32),
            ],
        ),
        out_shape=[
            jax.ShapeDtypeStruct((rows, BLK), jnp.float32),
            jax.ShapeDtypeStruct((copies, GB, BLK), jnp.float32),
        ],
        compiler_params=pltpu.CompilerParams(vmem_limit_bytes=VMEM),
        name="column_pass",
    )(picks, pieces, high, picks_t, exps, logits)


def row_pass(picks, pieces, high, picks_v, exps, logits, copies, log_ratio):
    groups = exps.shape[0] // PER
    rows = high.shape[0]
    return pl.pallas_call(
        functools.partial(row_kernel, copies, log_ratio),
        grid_spec=pltpu.PrefetchScalarGridSpec(
            num_scalar_prefetch=1,
            grid=(groups,),
            in_specs=[
                whole(pieces),
                whole(high),
                whole(picks_v),
                pl.BlockSpec((PER, *exps.shape[1:]), lambda g, _: (g, 0, 0)),
                pl.BlockSpec(memory_space=pl.ANY),
            ],
            out_specs=pl.BlockSpec((copies, rows, BLK), lambda g, _: (0, 0, 0)),
            scratch_shapes=[
                pltpu.VMEM((GB, BLK), jnp.float32),
                pltpu.VMEM((rows, CAP * BLK), jnp.float32),
                pltpu.VMEM((rows, BLK), jnp.float32),
                pltpu.SMEM((1,), jnp.float32),
                pltpu.VMEM((rows, BLK), jnp.float32),
                pltpu.VMEM((PER, *exps.shape[1:]), jnp.bfloat16),
                pltpu.VMEM((rows, BLK), jnp.float32),
                pltpu.VMEM((rows, BLK), jnp.float32),
            ],
        ),
        out_shape=jax.ShapeDtypeStruct((copies, rows, BLK), jnp.float32),
        compiler_params=pltpu.CompilerParams(vmem_limit_bytes=VMEM),
        name="row_pass",
    )(picks, pieces, high, picks_v, exps, logits)


def candidates(pattern, low_block):
    _, slots = pattern.shape
    first = jnp.sum((pattern < low_block).astype(jnp.int32), axis=1)
    position = first[:, None] + jnp.arange(8, dtype=jnp.int32)[None, :]
    here = position[:, :, None] == jnp.arange(slots, dtype=jnp.int32)[None, None, :]
    offset = pattern - low_block
    found = jnp.max(jnp.where(here, offset[:, None, :], -1), axis=2)
    fits = (found < GB) & (jnp.arange(8, dtype=jnp.int32)[None, :] < CAP)
    return jnp.where(fits, found, -1)


def ring_shift(array, axis, step):
    size = lax.axis_size(axis)
    return lax.ppermute(array, axis, [(k, (k + step) % size) for k in range(size)])


def combine_kernel(offset, sign, pieces_ref, out_ref):
    lse = pieces_ref[0] if pieces_ref.shape[0] == 1 else log_sum(pieces_ref)
    lse = offset + sign * lse
    for k in range(out_ref.shape[0]):
        out_ref[k] = lse


def combine(pieces, copies, offset=0.0, sign=1.0):
    return pl.pallas_call(
        functools.partial(combine_kernel, offset, sign),
        out_shape=jax.ShapeDtypeStruct((copies, *pieces.shape[1:]), jnp.float32),
        compiler_params=pltpu.CompilerParams(vmem_limit_bytes=VMEM),
        name="combine",
    )(pieces)


def shards(frames, codes, pattern):
    along, core = CODES
    chips, cores = lax.axis_size(along), lax.axis_size(core)
    chip, half = lax.axis_index(along), lax.axis_index(core)
    code_copies = chips * cores
    steps = ((0,), (1, chips - 1), (2,))
    came = {0: frames, 1: ring_shift(frames, along, 1), chips - 1: ring_shift(frames, along, -1)}
    feature_width = codes.shape[1]
    num_blocks = codes.shape[0] // BLK
    frame_count = pattern.shape[0]
    picked = candidates(pattern, lax.axis_index(CODES) * num_blocks)
    codes = codes.reshape(num_blocks, BLK, feature_width)
    places = {
        (k, mine): (((chip - k) % chips) * cores + (half + mine) % cores).reshape(1)
        for step in steps
        for k in step
        for mine in (0, 1)
    }
    picks, picked, picked_t, places = lax.optimization_barrier(
        (picked.reshape(-1), picked, picked.T, places)
    )
    frames_total = frame_count * BLK * lax.axis_size(FRAMES)
    codes_total = num_blocks * BLK * lax.axis_size(CODES)
    log_ratio = math.log(frames_total / codes_total)
    made = ()
    for step in steps:
        blocks = tuple(came[k] for k in step)
        if made:
            blocks, made = lax.optimization_barrier((blocks, made))
        other = tuple(ring_shift(block, core, 1) for block in blocks)
        for mine, group in enumerate((blocks, other)):
            for k, block in zip(step, group):
                made = make_tiles(picks, places[k, mine], block, codes, code_copies, made)
                if 2 not in came:
                    far, made = lax.optimization_barrier((frames, made))
                    came[2] = ring_shift(far, along, 2)
    exps, logits, high, lse = made
    first, second = FRAMES
    pieces = combine(lse[None], code_copies)
    for iteration in range(ITERS):
        pieces = lax.all_to_all(pieces, CODES, 0, 0, tiled=True)
        row_potential, pieces = column_pass(
            picks, pieces, high, picked_t, exps, logits, lax.axis_size(first)
        )
        pieces = lax.all_to_all(pieces, first, 0, 0, tiled=True)
        pieces = combine(pieces, lax.axis_size(second))
        pieces = lax.all_to_all(pieces, second, 0, 0, tiled=True)
        if iteration < ITERS - 1:
            pieces = row_pass(
                picks, pieces, high, picked, exps, logits, code_copies, log_ratio
            )
    col_potential = combine(pieces, 1, log_ratio, -1.0)
    return (row_potential.reshape(-1), col_potential.reshape(-1))


def solution(mesh):
    torus = Mesh(mesh.devices.reshape(4, 8, 4, 2), ("frames_0", "frames_1", "codes_0", "codes_1"))
    placed = (P(FRAMES_CODES, None), P(CODES, None), P(FRAMES, None))

    return jax.shard_map(
        shards, mesh=torus, in_specs=placed, out_specs=(P(FRAMES), P(CODES)), check_vma=False
    )
```

```python
import functools
import math

import jax
import jax.numpy as jnp
from jax import lax
from jax.experimental import pallas as pl
from jax.experimental.pallas import tpu as pltpu
from jax.sharding import Mesh
from jax.sharding import PartitionSpec as P


BLK = 128
GB = 64
CAP = 6
ITERS = 3
PER = 8
CODES = ("codes_0", "codes_1")
FRAMES = ("frames_0", "frames_1")
FRAMES_CODES = ("frames_0", "frames_1", "codes_0", "codes_1")

NEG_FILL = -1e30
NEG_ROW = -1e29
SMALL = 1e-26
VMEM = 14 * 1024 * 1024


def tiles_kernel(parts, picks, chunk, codes_ref, *refs):
    exp_ref, logit_ref, high_ref, lse_ref = refs[-4:]
    for b in range(PER):
        held = PER // parts
        at = (b % held) * BLK
        block = refs[b // held][at : at + BLK, :] * jnp.bfloat16(2.0)
        first = picks[(chunk[0] * PER + b) * 8]
        filled = []
        top = None
        for s in range(CAP):
            pick = picks[(chunk[0] * PER + b) * 8 + s]
            chosen = codes_ref[jnp.maximum(jnp.where(pick >= 0, pick, first), 0)]
            filled.append(jnp.where(pick >= 0, 1.0, 0.0))
            tile = lax.dot_general(
                chosen, block, (((1,), (1,)), ((), ())), preferred_element_type=jnp.float32
            )
            logit_ref[b, s * BLK : (s + 1) * BLK, :] = tile.astype(jnp.bfloat16)
            part = jnp.max(tile.reshape(BLK // 8, 8, BLK), axis=0)
            top = part if top is None else jnp.maximum(top, part)
        high = jnp.max(top, axis=0, keepdims=True).astype(jnp.bfloat16).astype(jnp.float32)
        total = None
        for s in range(CAP):
            tile = logit_ref[b, s * BLK : (s + 1) * BLK, :].astype(jnp.float32)
            terms = jnp.exp(tile - high)
            exp_ref[b, s * BLK : (s + 1) * BLK, :] = terms.astype(jnp.bfloat16)
            part = jnp.sum(terms.reshape(BLK // 8, 8, BLK), axis=0) * filled[s]
            total = part if total is None else total + part
        total = jnp.sum(total, axis=0, keepdims=True)
        high_ref[b : b + 1, :] = jnp.where(first >= 0, high, NEG_ROW)
        lse_ref[b : b + 1, :] = jnp.where(first >= 0, high + jnp.log(total), NEG_FILL)


def make_tiles(picks, chunk, frames, codes, chunks, before):
    parts = len(frames)
    tile_rows = CAP * BLK
    tiles = pl.BlockSpec((PER, tile_rows, BLK), lambda g, _, chunk: (chunk[0], 0, 0))
    lines = pl.BlockSpec((PER, BLK), lambda g, _, chunk: (chunk[0], 0))
    tiles_shape = jax.ShapeDtypeStruct((chunks * PER, tile_rows, BLK), jnp.bfloat16)
    lines_shape = jax.ShapeDtypeStruct((chunks * PER, BLK), jnp.float32)
    return pl.pallas_call(
        functools.partial(tiles_kernel, parts),
        grid_spec=pltpu.PrefetchScalarGridSpec(
            num_scalar_prefetch=2,
            grid=(1,),
            in_specs=[
                pl.BlockSpec(codes.shape, lambda g, *_: (0, 0, 0), pipeline_mode=pl.Buffered(1)),
                *[
                    pl.BlockSpec(part.shape, lambda g, *_: (0, 0), pipeline_mode=pl.Buffered(1))
                    for part in frames
                ],
                *[pl.BlockSpec(memory_space=pl.ANY) for _ in before],
            ],
            out_specs=[tiles, tiles, lines, lines],
        ),
        out_shape=[tiles_shape, tiles_shape, lines_shape, lines_shape],
        input_output_aliases={3 + parts + k: k for k in range(len(before))},
        cost_estimate=pl.CostEstimate(
            flops=2 * tile_rows * PER * BLK * codes.shape[2],
            bytes_accessed=4 * tile_rows * PER * BLK,
            transcendentals=tile_rows * PER * BLK,
        ),
        compiler_params=pltpu.CompilerParams(vmem_limit_bytes=VMEM),
        name="make_tiles",
    )(picks, chunk, codes, *frames, *before)


def halves_kernel(left_ref, right_ref, upper_ref, lower_ref):
    half = upper_ref.shape[0]
    upper_ref[...] = left_ref[:half, :]
    lower_ref[...] = right_ref[half:, :]


def halves(left, right):
    shape = jax.ShapeDtypeStruct((left.shape[0] // 2, left.shape[1]), left.dtype)
    return pl.pallas_call(
        halves_kernel,
        out_shape=[shape, shape],
        compiler_params=pltpu.CompilerParams(vmem_limit_bytes=VMEM),
        name="halves",
    )(left, right)


def pair(tiles_ref, q):
    return jnp.concatenate([tiles_ref[2 * q], tiles_ref[2 * q + 1]], axis=1)


def log_sum(pieces):
    high = pieces[0]
    for piece in pieces[1:]:
        high = jnp.maximum(high, piece)
    total = jnp.exp(pieces[0] - high)
    for piece in pieces[1:]:
        total = total + jnp.exp(piece - high)
    return high + jnp.log(total)


def arrived(refs, kept_ref=None):
    if len(refs) == 1:
        return [refs[0][k] for k in range(refs[0].shape[0])]
    pieces = []
    for k in range(refs[0].shape[0]):
        pieces.append(refs[0][k] + refs[1][k].astype(jnp.float32))
        if kept_ref is not None:
            kept_ref[k] = pieces[k]
    return pieces


def send(piece, out_ref, own_ref=None, kept_ref=None):
    if own_ref is None:
        change = piece
        if kept_ref is not None:
            kept_ref[...] = piece
    else:
        change = (piece - own_ref[...]).astype(jnp.bfloat16)
        kept_ref[...] = own_ref[...] + change.astype(jnp.float32)
    for k in range(out_ref.shape[0]):
        out_ref[k] = change


def split_dot(selector, values):
    upper = values.astype(jnp.bfloat16)
    lower = (values - upper.astype(jnp.float32)).astype(jnp.bfloat16)
    return jnp.dot(selector, upper, preferred_element_type=jnp.float32) + jnp.dot(
        selector, lower, preferred_element_type=jnp.float32
    )


def stable_pass(picks, logit_ref, shift_ref, out_ref, block_ref, high_ref, total_ref, by_code):
    high_ref[...] = jnp.full_like(high_ref, NEG_FILL)
    total_ref[...] = jnp.zeros_like(total_ref)

    def one_group(g, _):
        pltpu.sync_copy(logit_ref.at[pl.ds(g * PER, PER)], block_ref)

        def one_tile(index, _):
            b = index // CAP
            s = index - b * CAP
            row = g * PER + b
            pick = picks[row * 8 + s]

            @pl.when(pick >= 0)
            def _():
                rows = pl.ds(pl.multiple_of(s * BLK, BLK), BLK)
                tile = block_ref[b, rows, :].astype(jnp.float32)
                if by_code:
                    tile = jnp.transpose(tile + shift_ref[pl.ds(row, 1), :])
                    at = pl.ds(pick, 1)
                else:
                    shift = jnp.broadcast_to(shift_ref[pl.ds(pick, 1), :], (BLK, BLK))
                    tile = tile + jnp.transpose(shift)
                    at = pl.ds(row, 1)
                before = high_ref[at, :]
                high = jnp.maximum(before, jnp.max(tile, axis=0, keepdims=True))
                total_ref[at, :] = total_ref[at, :] * jnp.exp(before - high) + jnp.sum(
                    jnp.exp(tile - high), axis=0, keepdims=True
                )
                high_ref[at, :] = high

            return 0

        lax.fori_loop(0, CAP * PER, one_tile, 0)
        return 0

    lax.fori_loop(0, logit_ref.shape[0] // PER, one_group, 0)
    total = total_ref[...]
    out_ref[...] = jnp.where(
        total > 0.0, high_ref[...] + jnp.log(jnp.maximum(total, 1e-37)), NEG_FILL
    )


def column_kernel(pieces, picks, *refs):
    piece_refs, (high_ref, picks_ref, exp_ref, logit_ref, row_ref, out_ref), refs = (
        refs[:pieces], refs[pieces : pieces + 6], refs[pieces + 6 :]
    )
    kept_ref = refs[0] if pieces == 2 else None
    scale_ref, sums_ref, peak_ref, lse_ref, block_ref, top_ref, total_ref = refs[-7:]
    group = pl.program_id(0)

    @pl.when(group == 0)
    def _():
        row = -log_sum(arrived(piece_refs, kept_ref))
        row_ref[...] = row
        weight = high_ref[...] + row
        peak = jnp.max(weight)
        peak_ref[0] = peak
        scale_ref[...] = jnp.exp(weight - peak)

    scale = scale_ref[pl.ds(pl.multiple_of(group * PER, PER), PER), :]
    wide = jnp.concatenate([scale] * PER, axis=1)
    lane_block = lax.broadcasted_iota(jnp.int32, wide.shape, 1) // BLK
    row_block = lax.broadcasted_iota(jnp.int32, wide.shape, 0)
    wide = jnp.where(lane_block == row_block, wide, 0.0).astype(jnp.bfloat16)
    sums = None
    for q in range(PER // 2):
        part = lax.dot_general(
            wide[:, 2 * q * BLK : 2 * (q + 1) * BLK],
            pair(exp_ref, q),
            (((1,), (1,)), ((), ())),
            preferred_element_type=jnp.float32,
        )
        sums = part if sums is None else sums + part
    sums_ref[pl.ds(pl.multiple_of(group * PER, PER), PER), :] = sums

    @pl.when(group == pl.num_programs(0) - 1)
    def _():
        blocks = lax.broadcasted_iota(jnp.int32, (GB, picks_ref.shape[1]), 0)
        total = jnp.zeros(lse_ref.shape, jnp.float32)
        used = jnp.zeros((GB, 1), jnp.float32)
        for s in range(CAP):
            hit = (picks_ref[s : s + 1, :] == blocks).astype(jnp.float32)
            used = used + jnp.sum(hit, axis=1, keepdims=True)
            total = total + split_dot(
                hit.astype(jnp.bfloat16), sums_ref[:, s * BLK : (s + 1) * BLK]
            )
        lse_ref[...] = jnp.where(
            total > 0.0, peak_ref[0] + jnp.log(jnp.maximum(total, 1e-37)), NEG_FILL
        )
        low = jnp.min(jnp.where(used > 0.0, total, 1.0))

        @pl.when(jnp.logical_not(low >= SMALL))
        def _():
            stable_pass(
                picks, logit_ref, row_ref, lse_ref, block_ref, top_ref, total_ref, True
            )

        send(lse_ref[...], out_ref)


def row_kernel(pieces, log_ratio, picks, *refs):
    piece_refs, (own_ref, high_ref, picks_ref, exp_ref, logit_ref, out_ref, sent_ref), refs = (
        refs[:pieces], refs[pieces : pieces + 7], refs[pieces + 7 :]
    )
    kept_ref = refs[0] if pieces == 2 else None
    col_ref, scale_ref, sums_ref, peak_ref, lse_ref, block_ref, top_ref, total_ref = refs[-8:]
    group = pl.program_id(0)

    @pl.when(group == 0)
    def _():
        col = log_ratio - log_sum(arrived(piece_refs, kept_ref))
        col_ref[...] = col
        peak = jnp.max(col)
        peak_ref[0] = peak
        scale = jnp.exp(col - peak).astype(jnp.bfloat16)
        blocks = lax.broadcasted_iota(jnp.int32, (picks_ref.shape[0], GB), 1)
        for s in range(CAP):
            hit = (picks_ref[:, s : s + 1] == blocks).astype(jnp.float32).astype(jnp.bfloat16)
            scale_ref[:, s * BLK : (s + 1) * BLK] = jnp.dot(
                hit, scale, preferred_element_type=jnp.float32
            )

    at = pl.ds(pl.multiple_of(group * PER, PER), PER)
    scale = scale_ref[at, :].astype(jnp.bfloat16)
    row_block = lax.broadcasted_iota(jnp.int32, (PER, BLK), 0)
    total = jnp.zeros((PER, BLK), jnp.float32)
    for q in range(PER // 2):
        wide = jnp.dot(scale, pair(exp_ref, q), preferred_element_type=jnp.float32)
        total = total + jnp.where(row_block == 2 * q, wide[:, :BLK], 0.0)
        total = total + jnp.where(row_block == 2 * q + 1, wide[:, BLK:], 0.0)
    sums_ref[at, :] = total

    @pl.when(group == pl.num_programs(0) - 1)
    def _():
        total = sums_ref[...]
        lse_ref[...] = jnp.where(
            total > 0.0,
            high_ref[...] + (peak_ref[0] + jnp.log(jnp.maximum(total, 1e-37))),
            NEG_FILL,
        )
        low = jnp.min(jnp.where(picks_ref[:, 0:1] >= 0, total, 1.0))

        @pl.when(jnp.logical_not(low >= SMALL))
        def _():
            stable_pass(
                picks, logit_ref, col_ref, lse_ref, block_ref, top_ref, total_ref, False
            )

        send(lse_ref[...], out_ref, own_ref, sent_ref)


def whole(array):
    zeros = (0,) * array.ndim
    return pl.BlockSpec(array.shape, lambda g, _: zeros, pipeline_mode=pl.Buffered(1))


def fixed(shape):
    zeros = (0,) * len(shape)
    return pl.BlockSpec(shape, lambda g, _: zeros)


def column_pass(picks, pieces, high, picks_t, exps, logits, copies):
    groups = exps.shape[0] // PER
    rows = high.shape[0]
    kept = pieces[:1] if len(pieces) == 2 else ()
    outs = [
        jax.ShapeDtypeStruct((rows, BLK), jnp.float32),
        jax.ShapeDtypeStruct((copies, GB, BLK), jnp.float32),
        *[jax.ShapeDtypeStruct(piece.shape, piece.dtype) for piece in kept],
    ]
    return pl.pallas_call(
        functools.partial(column_kernel, len(pieces)),
        grid_spec=pltpu.PrefetchScalarGridSpec(
            num_scalar_prefetch=1,
            grid=(groups,),
            in_specs=[
                *[whole(piece) for piece in pieces],
                whole(high),
                whole(picks_t),
                pl.BlockSpec((PER, *exps.shape[1:]), lambda g, _: (g, 0, 0)),
                pl.BlockSpec(memory_space=pl.ANY),
            ],
            out_specs=[fixed(out.shape) for out in outs],
            scratch_shapes=[
                pltpu.VMEM((rows, BLK), jnp.float32),
                pltpu.VMEM((rows, CAP * BLK), jnp.float32),
                pltpu.SMEM((1,), jnp.float32),
                pltpu.VMEM((GB, BLK), jnp.float32),
                pltpu.VMEM((PER, *exps.shape[1:]), jnp.bfloat16),
                pltpu.VMEM((GB, BLK), jnp.float32),
                pltpu.VMEM((GB, BLK), jnp.float32),
            ],
        ),
        out_shape=outs,
        compiler_params=pltpu.CompilerParams(vmem_limit_bytes=VMEM),
        name="column_pass",
    )(picks, *pieces, high, picks_t, exps, logits)


def row_pass(picks, pieces, own, high, picks_v, exps, logits, copies, log_ratio):
    groups = exps.shape[0] // PER
    rows = high.shape[0]
    kept = pieces[:1] if len(pieces) == 2 else ()
    outs = [
        jax.ShapeDtypeStruct((copies, rows, BLK), jnp.bfloat16),
        jax.ShapeDtypeStruct((rows, BLK), jnp.float32),
        *[jax.ShapeDtypeStruct(piece.shape, piece.dtype) for piece in kept],
    ]
    return pl.pallas_call(
        functools.partial(row_kernel, len(pieces), log_ratio),
        grid_spec=pltpu.PrefetchScalarGridSpec(
            num_scalar_prefetch=1,
            grid=(groups,),
            in_specs=[
                *[whole(piece) for piece in pieces],
                whole(own),
                whole(high),
                whole(picks_v),
                pl.BlockSpec((PER, *exps.shape[1:]), lambda g, _: (g, 0, 0)),
                pl.BlockSpec(memory_space=pl.ANY),
            ],
            out_specs=[fixed(out.shape) for out in outs],
            scratch_shapes=[
                pltpu.VMEM((GB, BLK), jnp.float32),
                pltpu.VMEM((rows, CAP * BLK), jnp.float32),
                pltpu.VMEM((rows, BLK), jnp.float32),
                pltpu.SMEM((1,), jnp.float32),
                pltpu.VMEM((rows, BLK), jnp.float32),
                pltpu.VMEM((PER, *exps.shape[1:]), jnp.bfloat16),
                pltpu.VMEM((rows, BLK), jnp.float32),
                pltpu.VMEM((rows, BLK), jnp.float32),
            ],
        ),
        out_shape=outs,
        compiler_params=pltpu.CompilerParams(vmem_limit_bytes=VMEM),
        name="row_pass",
    )(picks, *pieces, own, high, picks_v, exps, logits)


def candidates(pattern, low_block):
    _, slots = pattern.shape
    first = jnp.sum((pattern < low_block).astype(jnp.int32), axis=1)
    position = first[:, None] + jnp.arange(8, dtype=jnp.int32)[None, :]
    here = position[:, :, None] == jnp.arange(slots, dtype=jnp.int32)[None, None, :]
    offset = pattern - low_block
    found = jnp.max(jnp.where(here, offset[:, None, :], -1), axis=2)
    fits = (found < GB) & (jnp.arange(8, dtype=jnp.int32)[None, :] < CAP)
    return jnp.where(fits, found, -1)


def ring_shift(array, axis, step):
    size = lax.axis_size(axis)
    return lax.ppermute(array, axis, [(k, (k + step) % size) for k in range(size)])


def combine_kernel(counts, offset, sign, *refs):
    pieces, olds = counts
    lse = log_sum(arrived(refs[:pieces]))
    old_refs, out_ref, kept_refs = (
        refs[pieces : pieces + olds], refs[pieces + olds], refs[pieces + olds + 1 :]
    )
    own_ref, kept_ref = (*old_refs, None)[0], (*kept_refs, None)[0]
    send(offset + sign * lse, out_ref, own_ref, kept_ref)


def combine(pieces, copies, own=None, offset=0.0, sign=1.0):
    lines = pieces[0].shape[1:]
    olds = () if own is None else (own,)
    kind = jnp.bfloat16 if olds else jnp.float32
    return pl.pallas_call(
        functools.partial(combine_kernel, (len(pieces), len(olds)), offset, sign),
        out_shape=[
            jax.ShapeDtypeStruct((copies, *lines), kind),
            jax.ShapeDtypeStruct(lines, jnp.float32),
        ],
        compiler_params=pltpu.CompilerParams(vmem_limit_bytes=VMEM),
        name="combine",
    )(*pieces, *olds)


def shards(frames, codes, pattern):
    along, core = CODES
    chips, cores = lax.axis_size(along), lax.axis_size(core)
    chip, half = lax.axis_index(along), lax.axis_index(core)
    code_copies = chips * cores
    from_left, from_right = ring_shift(frames, along, 1), ring_shift(frames, along, -1)
    feature_width = codes.shape[1]
    num_blocks = codes.shape[0] // BLK
    frame_count = pattern.shape[0]
    picked = candidates(pattern, lax.axis_index(CODES) * num_blocks)
    codes = codes.reshape(num_blocks, BLK, feature_width)
    places = {
        (k, mine): (((chip - k) % chips) * cores + (half + mine) % cores).reshape(1)
        for k in (0, 1, chips - 1, 2)
        for mine in (0, 1)
    }
    picks, picked, picked_t, places = lax.optimization_barrier(
        (picked.reshape(-1), picked, picked.T, places)
    )
    frames_total = frame_count * BLK * lax.axis_size(FRAMES)
    codes_total = num_blocks * BLK * lax.axis_size(CODES)
    log_ratio = math.log(frames_total / codes_total)
    made = ()

    def use(made, k, mine, *parts):
        return make_tiles(picks, places[k, mine], parts, codes, code_copies, made)

    other = ring_shift(frames, core, 1)
    made = use(made, 0, 0, frames)
    made = use(made, 0, 1, other)
    from_left, from_right, made = lax.optimization_barrier((from_left, from_right, made))
    upper, lower = halves(from_left, from_right)
    upper = ring_shift(upper, along, 1)
    lower = ring_shift(lower, along, -1)
    swapped = tuple(ring_shift(block, core, 1) for block in (from_left, from_right))
    made = use(made, 1, 0, from_left)
    made = use(made, chips - 1, 0, from_right)
    made = use(made, 1, 1, swapped[0])
    made = use(made, chips - 1, 1, swapped[1])
    upper, lower, made = lax.optimization_barrier((upper, lower, made))
    swapped = tuple(ring_shift(block, core, 1) for block in (upper, lower))
    made = use(made, 2, 0, upper, lower)
    made = use(made, 2, 1, *swapped)
    exps, logits, high, lse = made
    first, second = FRAMES

    def exchange(pieces, axes):
        return lax.all_to_all(pieces, axes, 0, 0, tiled=True)

    pieces, row_sent = combine((lse[None],), code_copies)
    rows = (exchange(pieces, CODES),)
    cols = ()
    col_sent = None
    for iteration in range(ITERS):
        row_potential, pieces, *kept = column_pass(
            picks, rows, high, picked_t, exps, logits, lax.axis_size(first)
        )
        rows = tuple(kept) or rows
        pieces = exchange(pieces, first)
        pieces, col_sent = combine((pieces,), lax.axis_size(second), col_sent)
        cols = (*cols[:1], exchange(pieces, second))
        if iteration < ITERS - 1:
            pieces, row_sent, *kept = row_pass(
                picks, cols, row_sent, high, picked, exps, logits, code_copies, log_ratio
            )
            cols = tuple(kept) or cols
            rows = (rows[0], exchange(pieces, CODES))
    _, col_potential = combine(cols, 1, None, log_ratio, -1.0)
    return (row_potential.reshape(-1), col_potential.reshape(-1))


def solution(mesh):
    torus = Mesh(mesh.devices.reshape(4, 8, 4, 2), ("frames_0", "frames_1", "codes_0", "codes_1"))
    placed = (P(FRAMES_CODES, None), P(CODES, None), P(FRAMES, None))

    return jax.shard_map(
        shards, mesh=torus, in_specs=placed, out_specs=(P(FRAMES), P(CODES)), check_vma=False
    )
```

```python
import functools
import math

import jax
import jax.numpy as jnp
from jax import lax
from jax.experimental import pallas as pl
from jax.experimental.pallas import tpu as pltpu
from jax.sharding import Mesh
from jax.sharding import PartitionSpec as P


BLK = 128
GB = 64
CAP = 6
ITERS = 3
PER = 8
STEP = 4
CODES = ("codes_0", "codes_1")
FRAMES = ("frames_0", "frames_1")
FRAMES_CODES = ("frames_0", "frames_1", "codes_0", "codes_1")

NEG_FILL = -1e30
NEG_ROW = -1e29
SMALL = 1e-26
VMEM = 14 * 1024 * 1024


def tiles_kernel(parts, picks, chunk, codes_ref, *refs):
    exp_ref, logit_ref, high_ref, lse_ref = refs[-4:]
    for b in range(PER):
        held = PER // parts
        at = (b % held) * BLK
        block = refs[b // held][at : at + BLK, :] * jnp.bfloat16(2.0)
        first = picks[(chunk[0] * PER + b) * 8]
        chosen, filled = [], []
        for s in range(CAP):
            pick = picks[(chunk[0] * PER + b) * 8 + s]
            chosen.append(codes_ref[jnp.maximum(jnp.where(pick >= 0, pick, first), 0)])
            filled.append(jnp.where(pick >= 0, 1.0, 0.0))
        top = None
        for s in range(0, CAP, 3):
            three = lax.dot_general(
                jnp.concatenate(chosen[s : s + 3], axis=0),
                block,
                (((1,), (1,)), ((), ())),
                preferred_element_type=jnp.float32,
            )
            logit_ref[b, s * BLK : (s + 3) * BLK, :] = three.astype(jnp.bfloat16)
            part = jnp.max(three.reshape(3 * BLK // 8, 8, BLK), axis=0)
            top = part if top is None else jnp.maximum(top, part)
        high = jnp.max(top, axis=0, keepdims=True).astype(jnp.bfloat16).astype(jnp.float32)
        total = None
        for s in range(CAP):
            tile = logit_ref[b, s * BLK : (s + 1) * BLK, :].astype(jnp.float32)
            terms = jnp.exp(tile - high)
            exp_ref[b, s * BLK : (s + 1) * BLK, :] = terms.astype(jnp.bfloat16)
            part = jnp.sum(terms.reshape(BLK // 8, 8, BLK), axis=0) * filled[s]
            total = part if total is None else total + part
        total = jnp.sum(total, axis=0, keepdims=True)
        high_ref[b : b + 1, :] = jnp.where(first >= 0, high, NEG_ROW)
        lse_ref[b : b + 1, :] = jnp.where(first >= 0, high + jnp.log(total), NEG_FILL)


def make_tiles(picks, chunk, frames, codes, chunks, before):
    parts = len(frames)
    tile_rows = CAP * BLK
    tiles = pl.BlockSpec((PER, tile_rows, BLK), lambda g, _, chunk: (chunk[0], 0, 0))
    lines = pl.BlockSpec((PER, BLK), lambda g, _, chunk: (chunk[0], 0))
    tiles_shape = jax.ShapeDtypeStruct((chunks * PER, tile_rows, BLK), jnp.bfloat16)
    lines_shape = jax.ShapeDtypeStruct((chunks * PER, BLK), jnp.float32)
    return pl.pallas_call(
        functools.partial(tiles_kernel, parts),
        grid_spec=pltpu.PrefetchScalarGridSpec(
            num_scalar_prefetch=2,
            grid=(1,),
            in_specs=[
                pl.BlockSpec(codes.shape, lambda g, *_: (0, 0, 0), pipeline_mode=pl.Buffered(1)),
                *[
                    pl.BlockSpec(part.shape, lambda g, *_: (0, 0), pipeline_mode=pl.Buffered(1))
                    for part in frames
                ],
                *[pl.BlockSpec(memory_space=pl.ANY) for _ in before],
            ],
            out_specs=[tiles, tiles, lines, lines],
        ),
        out_shape=[tiles_shape, tiles_shape, lines_shape, lines_shape],
        input_output_aliases={3 + parts + k: k for k in range(len(before))},
        cost_estimate=pl.CostEstimate(
            flops=2 * tile_rows * PER * BLK * codes.shape[2],
            bytes_accessed=4 * tile_rows * PER * BLK,
            transcendentals=tile_rows * PER * BLK,
        ),
        compiler_params=pltpu.CompilerParams(vmem_limit_bytes=VMEM),
        name="make_tiles",
    )(picks, chunk, codes, *frames, *before)


def pair(tiles_ref, q):
    return jnp.concatenate([tiles_ref[2 * q], tiles_ref[2 * q + 1]], axis=1)


def log_sum(pieces):
    high = pieces[0]
    for piece in pieces[1:]:
        high = jnp.maximum(high, piece)
    total = jnp.exp(pieces[0] - high)
    for piece in pieces[1:]:
        total = total + jnp.exp(piece - high)
    return high + jnp.log(total)


def arrived(refs, kept_ref=None):
    if len(refs) == 1:
        return [refs[0][k] for k in range(refs[0].shape[0])]
    pieces = []
    for k in range(refs[0].shape[0]):
        pieces.append(refs[0][k] + refs[1][k].astype(jnp.float32))
        if kept_ref is not None:
            kept_ref[k] = pieces[k]
    return pieces


def send(piece, out_ref, own_ref=None, kept_ref=None):
    if own_ref is None:
        change = piece
        if kept_ref is not None:
            kept_ref[...] = piece
    else:
        change = (piece - own_ref[...]).astype(jnp.bfloat16)
        if kept_ref is not None:
            kept_ref[...] = own_ref[...] + change.astype(jnp.float32)
    for k in range(out_ref.shape[0]):
        out_ref[k] = change


def split_dot(selector, values):
    upper = values.astype(jnp.bfloat16)
    lower = (values - upper.astype(jnp.float32)).astype(jnp.bfloat16)
    return jnp.dot(selector, upper, preferred_element_type=jnp.float32) + jnp.dot(
        selector, lower, preferred_element_type=jnp.float32
    )


def stable_pass(picks, logit_ref, shift_ref, out_ref, block_ref, high_ref, total_ref, by_code):
    high_ref[...] = jnp.full_like(high_ref, NEG_FILL)
    total_ref[...] = jnp.zeros_like(total_ref)

    def one_group(g, _):
        pltpu.sync_copy(logit_ref.at[pl.ds(g * PER, PER)], block_ref)

        def one_tile(index, _):
            b = index // CAP
            s = index - b * CAP
            row = g * PER + b
            pick = picks[row * 8 + s]

            @pl.when(pick >= 0)
            def _():
                rows = pl.ds(pl.multiple_of(s * BLK, BLK), BLK)
                tile = block_ref[b, rows, :].astype(jnp.float32)
                if by_code:
                    tile = jnp.transpose(tile + shift_ref[pl.ds(row, 1), :])
                    at = pl.ds(pick, 1)
                else:
                    shift = jnp.broadcast_to(shift_ref[pl.ds(pick, 1), :], (BLK, BLK))
                    tile = tile + jnp.transpose(shift)
                    at = pl.ds(row, 1)
                before = high_ref[at, :]
                high = jnp.maximum(before, jnp.max(tile, axis=0, keepdims=True))
                total_ref[at, :] = total_ref[at, :] * jnp.exp(before - high) + jnp.sum(
                    jnp.exp(tile - high), axis=0, keepdims=True
                )
                high_ref[at, :] = high

            return 0

        lax.fori_loop(0, CAP * PER, one_tile, 0)
        return 0

    lax.fori_loop(0, logit_ref.shape[0] // PER, one_group, 0)
    total = total_ref[...]
    out_ref[...] = jnp.where(
        total > 0.0, high_ref[...] + jnp.log(jnp.maximum(total, 1e-37)), NEG_FILL
    )


def column_kernel(pieces, last, picks, *refs):
    piece_refs, (high_ref, picks_ref, exp_ref, logit_ref, out_ref), refs = (
        refs[:pieces], refs[pieces : pieces + 5], refs[pieces + 5 :]
    )
    kept_ref = refs[0] if pieces == 2 and not last else None
    row_ref, scale_ref, sums_ref, peak_ref, lse_ref, block_ref, top_ref, total_ref = refs[-8:]
    if last:
        row_ref = refs[0]
    group = pl.program_id(0)

    @pl.when(group == 0)
    def _():
        row = -log_sum(arrived(piece_refs, kept_ref))
        row_ref[...] = row
        weight = high_ref[...] + row
        peak = jnp.max(weight)
        peak_ref[0] = peak
        scale_ref[...] = jnp.exp(weight - peak)

    for part in range(STEP):
        at = pl.ds(pl.multiple_of((group * STEP + part) * PER, PER), PER)
        wide = jnp.concatenate([scale_ref[at, :]] * PER, axis=1)
        lane_block = lax.broadcasted_iota(jnp.int32, wide.shape, 1) // BLK
        row_block = lax.broadcasted_iota(jnp.int32, wide.shape, 0)
        wide = jnp.where(lane_block == row_block, wide, 0.0).astype(jnp.bfloat16)
        sums = None
        for q in range(PER // 2):
            product = lax.dot_general(
                wide[:, 2 * q * BLK : 2 * (q + 1) * BLK],
                pair(exp_ref, part * PER // 2 + q),
                (((1,), (1,)), ((), ())),
                preferred_element_type=jnp.float32,
            )
            sums = product if sums is None else sums + product
        sums_ref[at, :] = sums

    @pl.when(group == pl.num_programs(0) - 1)
    def _():
        blocks = lax.broadcasted_iota(jnp.int32, (GB, picks_ref.shape[1]), 0)
        total = jnp.zeros(lse_ref.shape, jnp.float32)
        used = jnp.zeros((GB, 1), jnp.float32)
        for s in range(CAP):
            hit = (picks_ref[s : s + 1, :] == blocks).astype(jnp.float32)
            used = used + jnp.sum(hit, axis=1, keepdims=True)
            total = total + split_dot(
                hit.astype(jnp.bfloat16), sums_ref[:, s * BLK : (s + 1) * BLK]
            )
        lse_ref[...] = jnp.where(
            total > 0.0, peak_ref[0] + jnp.log(jnp.maximum(total, 1e-37)), NEG_FILL
        )
        low = jnp.min(jnp.where(used > 0.0, total, 1.0))

        @pl.when(jnp.logical_not(low >= SMALL))
        def _():
            stable_pass(
                picks, logit_ref, row_ref, lse_ref, block_ref, top_ref, total_ref, True
            )

        send(lse_ref[...], out_ref)


def row_kernel(pieces, keep, log_ratio, picks, *refs):
    piece_refs, (own_ref, high_ref, picks_ref, exp_ref, logit_ref, out_ref), refs = (
        refs[:pieces], refs[pieces : pieces + 6], refs[pieces + 6 :]
    )
    sent_ref = refs[0] if keep else None
    kept_ref = refs[keep] if pieces == 2 else None
    col_ref, scale_ref, sums_ref, peak_ref, lse_ref, block_ref, top_ref, total_ref = refs[-8:]
    group = pl.program_id(0)

    @pl.when(group == 0)
    def _():
        col = log_ratio - log_sum(arrived(piece_refs, kept_ref))
        col_ref[...] = col
        peak = jnp.max(col)
        peak_ref[0] = peak
        scale = jnp.exp(col - peak).astype(jnp.bfloat16)
        blocks = lax.broadcasted_iota(jnp.int32, (picks_ref.shape[0], GB), 1)
        for s in range(CAP):
            hit = (picks_ref[:, s : s + 1] == blocks).astype(jnp.float32).astype(jnp.bfloat16)
            scale_ref[:, s * BLK : (s + 1) * BLK] = jnp.dot(
                hit, scale, preferred_element_type=jnp.float32
            )

    for part in range(STEP):
        at = pl.ds(pl.multiple_of((group * STEP + part) * PER, PER), PER)
        scale = scale_ref[at, :].astype(jnp.bfloat16)
        row_block = lax.broadcasted_iota(jnp.int32, (PER, BLK), 0)
        total = jnp.zeros((PER, BLK), jnp.float32)
        for q in range(PER // 2):
            wide = jnp.dot(
                scale, pair(exp_ref, part * PER // 2 + q), preferred_element_type=jnp.float32
            )
            total = total + jnp.where(row_block == 2 * q, wide[:, :BLK], 0.0)
            total = total + jnp.where(row_block == 2 * q + 1, wide[:, BLK:], 0.0)
        sums_ref[at, :] = total

    @pl.when(group == pl.num_programs(0) - 1)
    def _():
        total = sums_ref[...]
        lse_ref[...] = jnp.where(
            total > 0.0,
            high_ref[...] + (peak_ref[0] + jnp.log(jnp.maximum(total, 1e-37))),
            NEG_FILL,
        )
        low = jnp.min(jnp.where(picks_ref[:, 0:1] >= 0, total, 1.0))

        @pl.when(jnp.logical_not(low >= SMALL))
        def _():
            stable_pass(
                picks, logit_ref, col_ref, lse_ref, block_ref, top_ref, total_ref, False
            )

        send(lse_ref[...], out_ref, own_ref, sent_ref)


def whole(array):
    zeros = (0,) * array.ndim
    return pl.BlockSpec(array.shape, lambda g, _: zeros, pipeline_mode=pl.Buffered(1))


def fixed(shape):
    zeros = (0,) * len(shape)
    return pl.BlockSpec(shape, lambda g, _: zeros)


def column_pass(picks, pieces, high, picks_t, exps, logits, copies, last):
    groups = exps.shape[0] // PER
    rows = high.shape[0]
    kept = pieces[:1] if len(pieces) == 2 else ()
    if last:
        kept = (high,)
    outs = [
        jax.ShapeDtypeStruct((copies, GB, BLK), jnp.float32),
        *[jax.ShapeDtypeStruct(piece.shape, piece.dtype) for piece in kept],
    ]
    return pl.pallas_call(
        functools.partial(column_kernel, len(pieces), last),
        grid_spec=pltpu.PrefetchScalarGridSpec(
            num_scalar_prefetch=1,
            grid=(groups // STEP,),
            in_specs=[
                *[whole(piece) for piece in pieces],
                whole(high),
                whole(picks_t),
                pl.BlockSpec((STEP * PER, *exps.shape[1:]), lambda g, _: (g, 0, 0)),
                pl.BlockSpec(memory_space=pl.ANY),
            ],
            out_specs=[fixed(out.shape) for out in outs],
            scratch_shapes=[
                pltpu.VMEM((rows, BLK), jnp.float32),
                pltpu.VMEM((rows, BLK), jnp.float32),
                pltpu.VMEM((rows, CAP * BLK), jnp.float32),
                pltpu.SMEM((1,), jnp.float32),
                pltpu.VMEM((GB, BLK), jnp.float32),
                pltpu.VMEM((PER, *exps.shape[1:]), jnp.bfloat16),
                pltpu.VMEM((GB, BLK), jnp.float32),
                pltpu.VMEM((GB, BLK), jnp.float32),
            ],
        ),
        out_shape=outs,
        compiler_params=pltpu.CompilerParams(vmem_limit_bytes=VMEM),
        name="column_pass",
    )(picks, *pieces, high, picks_t, exps, logits)


def row_pass(picks, pieces, own, high, picks_v, exps, logits, copies, log_ratio, keep):
    groups = exps.shape[0] // PER
    rows = high.shape[0]
    kept = pieces[:1] if len(pieces) == 2 else ()
    outs = [
        jax.ShapeDtypeStruct((copies, rows, BLK), jnp.bfloat16),
        *[jax.ShapeDtypeStruct((rows, BLK), jnp.float32) for _ in range(keep)],
        *[jax.ShapeDtypeStruct(piece.shape, piece.dtype) for piece in kept],
    ]
    return pl.pallas_call(
        functools.partial(row_kernel, len(pieces), keep, log_ratio),
        grid_spec=pltpu.PrefetchScalarGridSpec(
            num_scalar_prefetch=1,
            grid=(groups // STEP,),
            in_specs=[
                *[whole(piece) for piece in pieces],
                whole(own),
                whole(high),
                whole(picks_v),
                pl.BlockSpec((STEP * PER, *exps.shape[1:]), lambda g, _: (g, 0, 0)),
                pl.BlockSpec(memory_space=pl.ANY),
            ],
            out_specs=[fixed(out.shape) for out in outs],
            scratch_shapes=[
                pltpu.VMEM((GB, BLK), jnp.float32),
                pltpu.VMEM((rows, CAP * BLK), jnp.float32),
                pltpu.VMEM((rows, BLK), jnp.float32),
                pltpu.SMEM((1,), jnp.float32),
                pltpu.VMEM((rows, BLK), jnp.float32),
                pltpu.VMEM((PER, *exps.shape[1:]), jnp.bfloat16),
                pltpu.VMEM((rows, BLK), jnp.float32),
                pltpu.VMEM((rows, BLK), jnp.float32),
            ],
        ),
        out_shape=outs,
        compiler_params=pltpu.CompilerParams(vmem_limit_bytes=VMEM),
        name="row_pass",
    )(picks, *pieces, own, high, picks_v, exps, logits)


def candidates(pattern, low_block):
    _, slots = pattern.shape
    first = jnp.sum((pattern < low_block).astype(jnp.int32), axis=1)
    position = first[:, None] + jnp.arange(8, dtype=jnp.int32)[None, :]
    here = position[:, :, None] == jnp.arange(slots, dtype=jnp.int32)[None, None, :]
    offset = pattern - low_block
    found = jnp.max(jnp.where(here, offset[:, None, :], -1), axis=2)
    fits = (found < GB) & (jnp.arange(8, dtype=jnp.int32)[None, :] < CAP)
    return jnp.where(fits, found, -1)


def ring_shift(array, axis, step):
    size = lax.axis_size(axis)
    return lax.ppermute(array, axis, [(k, (k + step) % size) for k in range(size)])


def finish_kernel(log_ratio, kept_ref, change_ref, row_ref, row_out_ref, col_out_ref):
    row_out_ref[...] = row_ref[...]
    col_out_ref[...] = log_ratio - log_sum(arrived((kept_ref, change_ref)))


def finish(cols, row, log_ratio):
    return pl.pallas_call(
        functools.partial(finish_kernel, log_ratio),
        out_shape=[
            jax.ShapeDtypeStruct(row.shape, jnp.float32),
            jax.ShapeDtypeStruct(cols[0].shape[1:], jnp.float32),
        ],
        compiler_params=pltpu.CompilerParams(vmem_limit_bytes=VMEM),
        name="finish",
    )(*cols, row)


def combine_kernel(counts, *refs):
    pieces, olds = counts
    lse = log_sum(arrived(refs[:pieces]))
    old_refs, out_ref, kept_refs = (
        refs[pieces : pieces + olds], refs[pieces + olds], refs[pieces + olds + 1 :]
    )
    own_ref, kept_ref = (*old_refs, None)[0], (*kept_refs, None)[0]
    send(lse, out_ref, own_ref, kept_ref)


def combine(pieces, copies, own=None, keep=True):
    lines = pieces[0].shape[1:]
    olds = () if own is None else (own,)
    kind = jnp.bfloat16 if olds else jnp.float32
    return pl.pallas_call(
        functools.partial(combine_kernel, (len(pieces), len(olds))),
        out_shape=[
            jax.ShapeDtypeStruct((copies, *lines), kind),
            *[jax.ShapeDtypeStruct(lines, jnp.float32) for _ in range(keep)],
        ],
        compiler_params=pltpu.CompilerParams(vmem_limit_bytes=VMEM),
        name="combine",
    )(*pieces, *olds)


def shards(frames, codes, pattern):
    along, core = CODES
    chips, cores = lax.axis_size(along), lax.axis_size(core)
    chip, half = lax.axis_index(along), lax.axis_index(core)
    code_copies = chips * cores
    turn = 1 - 2 * half

    def crossing(step):
        there = []
        for k in range(chips):
            for c in range(cores):
                there.append((k * cores + c, (k + (1 - 2 * c) * step) % chips * cores + c))
        return there

    near = lax.ppermute(frames, CODES, crossing(1))
    feature_width = codes.shape[1]
    num_blocks = codes.shape[0] // BLK
    frame_count = pattern.shape[0]
    picked = candidates(pattern, lax.axis_index(CODES) * num_blocks)
    codes = codes.reshape(num_blocks, BLK, feature_width)
    places = {}
    for name, step in (("own", 0), ("near", -turn), ("back", turn), ("far", 2)):
        places[name, 0] = ((chip + step) % chips * cores + half).reshape(1)
        places[name, 1] = ((chip - step) % chips * cores + 1 - half).reshape(1)
    picks, picked, picked_t, places, late = lax.optimization_barrier(
        (picked.reshape(-1), picked, picked.T, places, frames)
    )
    back = lax.ppermute(late, CODES, crossing(-1))
    frames_total = frame_count * BLK * lax.axis_size(FRAMES)
    codes_total = num_blocks * BLK * lax.axis_size(CODES)
    log_ratio = math.log(frames_total / codes_total)
    made = ()

    def use(made, name, swapped, block):
        return make_tiles(picks, places[name, swapped], (block,), codes, code_copies, made)

    def swap(block):
        return ring_shift(block, core, 1)

    made = use(made, "own", 1, swap(frames))
    made = use(made, "own", 0, frames)
    near, made = lax.optimization_barrier((near, made))
    far = lax.ppermute(near, CODES, crossing(1))
    other = swap(near)
    made = use(made, "near", 0, near)
    made = use(made, "near", 1, other)
    back, made = lax.optimization_barrier((back, made))
    other = swap(back)
    made = use(made, "back", 0, back)
    made = use(made, "back", 1, other)
    far, made = lax.optimization_barrier((far, made))
    other = swap(far)
    made = use(made, "far", 0, far)
    made = use(made, "far", 1, other)
    exps, logits, high, lse = made
    first, second = FRAMES

    def exchange(pieces, axes):
        return lax.all_to_all(pieces, axes, 0, 0, tiled=True)

    pieces, row_sent = combine((lse[None],), code_copies)
    rows = (exchange(pieces, CODES),)
    cols = ()
    col_sent = None
    for iteration in range(ITERS):
        last = iteration == ITERS - 1
        pieces, *kept = column_pass(
            picks, rows, high, picked_t, exps, logits, lax.axis_size(first), last
        )
        rows = tuple(kept) or rows
        pieces = exchange(pieces, first)
        pieces, *kept = combine((pieces,), lax.axis_size(second), col_sent, keep=not last)
        col_sent = None if last else kept[0]
        cols = (*cols[:1], exchange(pieces, second))
        if not last:
            keep = iteration < ITERS - 2
            pieces, *kept = row_pass(
                picks, cols, row_sent, high, picked, exps, logits, code_copies, log_ratio, keep
            )
            if keep:
                row_sent, *kept = kept
            cols = tuple(kept) or cols
            rows = (rows[0], exchange(pieces, CODES))
    row_potential, col_potential = finish(cols, rows[0], log_ratio)
    return (row_potential.reshape(-1), col_potential.reshape(-1))


def solution(mesh):
    torus = Mesh(mesh.devices.reshape(4, 8, 4, 2), ("frames_0", "frames_1", "codes_0", "codes_1"))
    placed = (P(FRAMES_CODES, None), P(CODES, None), P(FRAMES, None))

    return jax.shard_map(
        shards, mesh=torus, in_specs=placed, out_specs=(P(FRAMES), P(CODES)), check_vma=False
    )
```

```python
import functools
import math

import jax
import jax.numpy as jnp
from jax import lax
from jax.experimental import pallas as pl
from jax.experimental.pallas import tpu as pltpu
from jax.sharding import Mesh
from jax.sharding import PartitionSpec as P


BLK = 128
GB = 64
CAP = 6
ITERS = 3
PER = 8
STEP = 4
CODES = ("codes_0", "codes_1")
FRAMES = ("frames_0", "frames_1")
FRAMES_CODES = ("frames_0", "frames_1", "codes_0", "codes_1")

NEG_FILL = -1e30
NEG_ROW = -1e29
SMALL = 1e-26
VMEM = 14 * 1024 * 1024


def tiles_kernel(parts, picks, chunk, codes_ref, *refs):
    exp_ref, logit_ref, high_ref, lse_ref = refs[-4:]
    for b in range(PER):
        held = PER // parts
        at = (b % held) * BLK
        block = refs[b // held][at : at + BLK, :] * jnp.bfloat16(2.0)
        first = picks[0, chunk[0] * PER + b]
        chosen, filled = [], []
        for s in range(CAP):
            pick = picks[s, chunk[0] * PER + b]
            chosen.append(codes_ref[jnp.maximum(jnp.where(pick >= 0, pick, first), 0)])
            filled.append(jnp.where(pick >= 0, 1.0, 0.0))
        top = None
        for s in range(0, CAP, 3):
            three = lax.dot_general(
                jnp.concatenate(chosen[s : s + 3], axis=0),
                block,
                (((1,), (1,)), ((), ())),
                preferred_element_type=jnp.float32,
            )
            logit_ref[b, s * BLK : (s + 3) * BLK, :] = three.astype(jnp.bfloat16)
            part = jnp.max(three.reshape(3 * BLK // 8, 8, BLK), axis=0)
            top = part if top is None else jnp.maximum(top, part)
        high = jnp.max(top, axis=0, keepdims=True).astype(jnp.bfloat16).astype(jnp.float32)
        total = None
        for s in range(CAP):
            tile = logit_ref[b, s * BLK : (s + 1) * BLK, :].astype(jnp.float32)
            terms = jnp.exp(tile - high)
            exp_ref[b, s * BLK : (s + 1) * BLK, :] = terms.astype(jnp.bfloat16)
            part = jnp.sum(terms.reshape(BLK // 8, 8, BLK), axis=0) * filled[s]
            total = part if total is None else total + part
        total = jnp.sum(total, axis=0, keepdims=True)
        high_ref[b : b + 1, :] = jnp.where(first >= 0, high, NEG_ROW)
        lse_ref[b : b + 1, :] = jnp.where(first >= 0, high + jnp.log(total), NEG_FILL)


def make_tiles(picks, chunk, frames, codes, chunks, before):
    parts = len(frames)
    tile_rows = CAP * BLK
    tiles = pl.BlockSpec((PER, tile_rows, BLK), lambda g, _, chunk: (chunk[0], 0, 0))
    lines = pl.BlockSpec((PER, BLK), lambda g, _, chunk: (chunk[0], 0))
    tiles_shape = jax.ShapeDtypeStruct((chunks * PER, tile_rows, BLK), jnp.bfloat16)
    lines_shape = jax.ShapeDtypeStruct((chunks * PER, BLK), jnp.float32)
    return pl.pallas_call(
        functools.partial(tiles_kernel, parts),
        grid_spec=pltpu.PrefetchScalarGridSpec(
            num_scalar_prefetch=2,
            grid=(1,),
            in_specs=[
                pl.BlockSpec(codes.shape, lambda g, *_: (0, 0, 0), pipeline_mode=pl.Buffered(1)),
                *[
                    pl.BlockSpec(part.shape, lambda g, *_: (0, 0), pipeline_mode=pl.Buffered(1))
                    for part in frames
                ],
                *[pl.BlockSpec(memory_space=pl.ANY) for _ in before],
            ],
            out_specs=[tiles, tiles, lines, lines],
        ),
        out_shape=[tiles_shape, tiles_shape, lines_shape, lines_shape],
        input_output_aliases={3 + parts + k: k for k in range(len(before))},
        cost_estimate=pl.CostEstimate(
            flops=2 * tile_rows * PER * BLK * codes.shape[2],
            bytes_accessed=4 * tile_rows * PER * BLK,
            transcendentals=tile_rows * PER * BLK,
        ),
        compiler_params=pltpu.CompilerParams(vmem_limit_bytes=VMEM),
        name="make_tiles",
    )(picks, chunk, codes, *frames, *before)


def pair(tiles_ref, q):
    return jnp.concatenate([tiles_ref[2 * q], tiles_ref[2 * q + 1]], axis=1)


def log_sum(pieces):
    high = pieces[0]
    for piece in pieces[1:]:
        high = jnp.maximum(high, piece)
    total = jnp.exp(pieces[0] - high)
    for piece in pieces[1:]:
        total = total + jnp.exp(piece - high)
    return high + jnp.log(total)


def arrived(refs, kept_ref=None):
    if len(refs) == 1:
        return [refs[0][k] for k in range(refs[0].shape[0])]
    pieces = []
    for k in range(refs[0].shape[0]):
        pieces.append(refs[0][k] + refs[1][k].astype(jnp.float32))
        if kept_ref is not None:
            kept_ref[k] = pieces[k]
    return pieces


def send(piece, out_ref, own_ref=None, kept_ref=None):
    if own_ref is None:
        change = piece
        if kept_ref is not None:
            kept_ref[...] = piece
    else:
        change = (piece - own_ref[...]).astype(jnp.bfloat16)
        if kept_ref is not None:
            kept_ref[...] = own_ref[...] + change.astype(jnp.float32)
    for k in range(out_ref.shape[0]):
        out_ref[k] = change


def split_dot(selector, values):
    upper = values.astype(jnp.bfloat16)
    lower = (values - upper.astype(jnp.float32)).astype(jnp.bfloat16)
    return jnp.dot(selector, upper, preferred_element_type=jnp.float32) + jnp.dot(
        selector, lower, preferred_element_type=jnp.float32
    )


def stable_pass(picks, logit_ref, shift_ref, out_ref, block_ref, high_ref, total_ref, by_code):
    high_ref[...] = jnp.full_like(high_ref, NEG_FILL)
    total_ref[...] = jnp.zeros_like(total_ref)

    def one_group(g, _):
        pltpu.sync_copy(logit_ref.at[pl.ds(g * PER, PER)], block_ref)

        def one_tile(index, _):
            b = index // CAP
            s = index - b * CAP
            row = g * PER + b
            pick = picks[s, row]

            @pl.when(pick >= 0)
            def _():
                rows = pl.ds(pl.multiple_of(s * BLK, BLK), BLK)
                tile = block_ref[b, rows, :].astype(jnp.float32)
                if by_code:
                    tile = jnp.transpose(tile + shift_ref[pl.ds(row, 1), :])
                    at = pl.ds(pick, 1)
                else:
                    shift = jnp.broadcast_to(shift_ref[pl.ds(pick, 1), :], (BLK, BLK))
                    tile = tile + jnp.transpose(shift)
                    at = pl.ds(row, 1)
                before = high_ref[at, :]
                high = jnp.maximum(before, jnp.max(tile, axis=0, keepdims=True))
                total_ref[at, :] = total_ref[at, :] * jnp.exp(before - high) + jnp.sum(
                    jnp.exp(tile - high), axis=0, keepdims=True
                )
                high_ref[at, :] = high

            return 0

        lax.fori_loop(0, CAP * PER, one_tile, 0)
        return 0

    lax.fori_loop(0, logit_ref.shape[0] // PER, one_group, 0)
    total = total_ref[...]
    out_ref[...] = jnp.where(
        total > 0.0, high_ref[...] + jnp.log(jnp.maximum(total, 1e-37)), NEG_FILL
    )


def column_kernel(pieces, last, picks, *refs):
    piece_refs, (high_ref, picks_ref, exp_ref, logit_ref, out_ref), refs = (
        refs[:pieces], refs[pieces : pieces + 5], refs[pieces + 5 :]
    )
    kept_ref = refs[0] if pieces == 2 and not last else None
    row_ref, scale_ref, sums_ref, peak_ref, lse_ref, block_ref, top_ref, total_ref = refs[-8:]
    if last:
        row_ref = refs[0]
    group = pl.program_id(0)

    @pl.when(group == 0)
    def _():
        row = -log_sum(arrived(piece_refs, kept_ref))
        row_ref[...] = row
        weight = high_ref[...] + row
        peak = jnp.max(weight)
        peak_ref[0] = peak
        scale_ref[...] = jnp.exp(weight - peak)

    for part in range(STEP):
        at = pl.ds(pl.multiple_of((group * STEP + part) * PER, PER), PER)
        wide = jnp.concatenate([scale_ref[at, :]] * PER, axis=1)
        lane_block = lax.broadcasted_iota(jnp.int32, wide.shape, 1) // BLK
        row_block = lax.broadcasted_iota(jnp.int32, wide.shape, 0)
        wide = jnp.where(lane_block == row_block, wide, 0.0).astype(jnp.bfloat16)
        sums = None
        for q in range(PER // 2):
            product = lax.dot_general(
                wide[:, 2 * q * BLK : 2 * (q + 1) * BLK],
                pair(exp_ref, part * PER // 2 + q),
                (((1,), (1,)), ((), ())),
                preferred_element_type=jnp.float32,
            )
            sums = product if sums is None else sums + product
        sums_ref[at, :] = sums

    @pl.when(group == pl.num_programs(0) - 1)
    def _():
        blocks = lax.broadcasted_iota(jnp.int32, (GB, picks_ref.shape[1]), 0)
        total = jnp.zeros(lse_ref.shape, jnp.float32)
        used = jnp.zeros((GB, 1), jnp.float32)
        for s in range(CAP):
            hit = (picks_ref[s : s + 1, :] == blocks).astype(jnp.float32)
            used = used + jnp.sum(hit, axis=1, keepdims=True)
            total = total + split_dot(
                hit.astype(jnp.bfloat16), sums_ref[:, s * BLK : (s + 1) * BLK]
            )
        lse_ref[...] = jnp.where(
            total > 0.0, peak_ref[0] + jnp.log(jnp.maximum(total, 1e-37)), NEG_FILL
        )
        low = jnp.min(jnp.where(used > 0.0, total, 1.0))

        @pl.when(jnp.logical_not(low >= SMALL))
        def _():
            stable_pass(
                picks, logit_ref, row_ref, lse_ref, block_ref, top_ref, total_ref, True
            )

        send(lse_ref[...], out_ref)


def row_kernel(pieces, keep, log_ratio, picks, *refs):
    piece_refs, (own_ref, high_ref, picks_ref, exp_ref, logit_ref, out_ref), refs = (
        refs[:pieces], refs[pieces : pieces + 6], refs[pieces + 6 :]
    )
    sent_ref = refs[0] if keep else None
    kept_ref = refs[keep] if pieces == 2 else None
    col_ref, scale_ref, sums_ref, peak_ref, lse_ref, block_ref, top_ref, total_ref = refs[-8:]
    group = pl.program_id(0)

    @pl.when(group == 0)
    def _():
        col = log_ratio - log_sum(arrived(piece_refs, kept_ref))
        col_ref[...] = col
        peak = jnp.max(col)
        peak_ref[0] = peak
        scale = jnp.exp(col - peak).astype(jnp.bfloat16)
        blocks = lax.broadcasted_iota(jnp.int32, (picks_ref.shape[0], GB), 1)
        for s in range(CAP):
            hit = (picks_ref[:, s : s + 1] == blocks).astype(jnp.float32).astype(jnp.bfloat16)
            scale_ref[:, s * BLK : (s + 1) * BLK] = jnp.dot(
                hit, scale, preferred_element_type=jnp.float32
            )

    for part in range(STEP):
        at = pl.ds(pl.multiple_of((group * STEP + part) * PER, PER), PER)
        scale = scale_ref[at, :].astype(jnp.bfloat16)
        row_block = lax.broadcasted_iota(jnp.int32, (PER, BLK), 0)
        total = jnp.zeros((PER, BLK), jnp.float32)
        for q in range(PER // 2):
            wide = jnp.dot(
                scale, pair(exp_ref, part * PER // 2 + q), preferred_element_type=jnp.float32
            )
            total = total + jnp.where(row_block == 2 * q, wide[:, :BLK], 0.0)
            total = total + jnp.where(row_block == 2 * q + 1, wide[:, BLK:], 0.0)
        sums_ref[at, :] = total

    @pl.when(group == pl.num_programs(0) - 1)
    def _():
        total = sums_ref[...]
        lse_ref[...] = jnp.where(
            total > 0.0,
            high_ref[...] + (peak_ref[0] + jnp.log(jnp.maximum(total, 1e-37))),
            NEG_FILL,
        )
        low = jnp.min(jnp.where(picks_ref[:, 0:1] >= 0, total, 1.0))

        @pl.when(jnp.logical_not(low >= SMALL))
        def _():
            stable_pass(
                picks, logit_ref, col_ref, lse_ref, block_ref, top_ref, total_ref, False
            )

        send(lse_ref[...], out_ref, own_ref, sent_ref)


def whole(array):
    zeros = (0,) * array.ndim
    return pl.BlockSpec(array.shape, lambda g, _: zeros, pipeline_mode=pl.Buffered(1))


def fixed(shape):
    zeros = (0,) * len(shape)
    return pl.BlockSpec(shape, lambda g, _: zeros)


def column_pass(picks, pieces, high, picks_t, exps, logits, copies, last):
    groups = exps.shape[0] // PER
    rows = high.shape[0]
    kept = pieces[:1] if len(pieces) == 2 else ()
    if last:
        kept = (high,)
    outs = [
        jax.ShapeDtypeStruct((copies, GB, BLK), jnp.float32),
        *[jax.ShapeDtypeStruct(piece.shape, piece.dtype) for piece in kept],
    ]
    return pl.pallas_call(
        functools.partial(column_kernel, len(pieces), last),
        grid_spec=pltpu.PrefetchScalarGridSpec(
            num_scalar_prefetch=1,
            grid=(groups // STEP,),
            in_specs=[
                *[whole(piece) for piece in pieces],
                whole(high),
                whole(picks_t),
                pl.BlockSpec((STEP * PER, *exps.shape[1:]), lambda g, _: (g, 0, 0)),
                pl.BlockSpec(memory_space=pl.ANY),
            ],
            out_specs=[fixed(out.shape) for out in outs],
            scratch_shapes=[
                pltpu.VMEM((rows, BLK), jnp.float32),
                pltpu.VMEM((rows, BLK), jnp.float32),
                pltpu.VMEM((rows, CAP * BLK), jnp.float32),
                pltpu.SMEM((1,), jnp.float32),
                pltpu.VMEM((GB, BLK), jnp.float32),
                pltpu.VMEM((PER, *exps.shape[1:]), jnp.bfloat16),
                pltpu.VMEM((GB, BLK), jnp.float32),
                pltpu.VMEM((GB, BLK), jnp.float32),
            ],
        ),
        out_shape=outs,
        compiler_params=pltpu.CompilerParams(vmem_limit_bytes=VMEM),
        name="column_pass",
    )(picks, *pieces, high, picks_t, exps, logits)


def row_pass(picks, pieces, own, high, picks_v, exps, logits, copies, log_ratio, keep):
    groups = exps.shape[0] // PER
    rows = high.shape[0]
    kept = pieces[:1] if len(pieces) == 2 else ()
    outs = [
        jax.ShapeDtypeStruct((copies, rows, BLK), jnp.bfloat16),
        *[jax.ShapeDtypeStruct((rows, BLK), jnp.float32) for _ in range(keep)],
        *[jax.ShapeDtypeStruct(piece.shape, piece.dtype) for piece in kept],
    ]
    return pl.pallas_call(
        functools.partial(row_kernel, len(pieces), keep, log_ratio),
        grid_spec=pltpu.PrefetchScalarGridSpec(
            num_scalar_prefetch=1,
            grid=(groups // STEP,),
            in_specs=[
                *[whole(piece) for piece in pieces],
                whole(own),
                whole(high),
                whole(picks_v),
                pl.BlockSpec((STEP * PER, *exps.shape[1:]), lambda g, _: (g, 0, 0)),
                pl.BlockSpec(memory_space=pl.ANY),
            ],
            out_specs=[fixed(out.shape) for out in outs],
            scratch_shapes=[
                pltpu.VMEM((GB, BLK), jnp.float32),
                pltpu.VMEM((rows, CAP * BLK), jnp.float32),
                pltpu.VMEM((rows, BLK), jnp.float32),
                pltpu.SMEM((1,), jnp.float32),
                pltpu.VMEM((rows, BLK), jnp.float32),
                pltpu.VMEM((PER, *exps.shape[1:]), jnp.bfloat16),
                pltpu.VMEM((rows, BLK), jnp.float32),
                pltpu.VMEM((rows, BLK), jnp.float32),
            ],
        ),
        out_shape=outs,
        compiler_params=pltpu.CompilerParams(vmem_limit_bytes=VMEM),
        name="row_pass",
    )(picks, *pieces, own, high, picks_v, exps, logits)


def tables_kernel(low_ref, pattern_ref, picked_ref, table_ref):
    low = low_ref[0]
    pattern = pattern_ref[...]
    rows, slots = pattern.shape
    first = jnp.sum(jnp.where(pattern < low, 1.0, 0.0), axis=1, keepdims=True)
    position = lax.broadcasted_iota(jnp.int32, (rows, slots), 1).astype(jnp.float32) - first
    offset = (pattern - low).astype(jnp.float32)
    lane = lax.broadcasted_iota(jnp.int32, (rows, BLK), 1)
    picked = jnp.full((rows, BLK), -1.0, jnp.float32)
    for s in range(CAP):
        found = jnp.max(jnp.where(position == s, offset, -1.0), axis=1, keepdims=True)
        found = jnp.where(found < GB, found, -1.0)
        picked = jnp.where(lane == s, found, picked)
    picked_ref[...] = picked[:, :8].astype(jnp.int32)
    table_ref[...] = jnp.transpose(picked)[:8, :].astype(jnp.int32)


def tables(low, pattern):
    rows = pattern.shape[0]
    near = pl.BlockSpec(memory_space=pltpu.VMEM)
    return pl.pallas_call(
        tables_kernel,
        in_specs=[pl.BlockSpec(memory_space=pltpu.SMEM), near],
        out_specs=[near, near],
        out_shape=[
            jax.ShapeDtypeStruct((rows, 8), jnp.int32),
            jax.ShapeDtypeStruct((8, rows), jnp.int32),
        ],
        cost_estimate=pl.CostEstimate(flops=0, bytes_accessed=1 << 23, transcendentals=0),
        compiler_params=pltpu.CompilerParams(vmem_limit_bytes=VMEM),
        name="tables",
    )(low, pattern)


def ring_shift(array, axis, step):
    size = lax.axis_size(axis)
    return lax.ppermute(array, axis, [(k, (k + step) % size) for k in range(size)])


def finish_kernel(log_ratio, kept_ref, change_ref, row_ref, row_out_ref, col_out_ref):
    row_out_ref[...] = row_ref[...]
    col_out_ref[...] = log_ratio - log_sum(arrived((kept_ref, change_ref)))


def finish(cols, row, log_ratio):
    return pl.pallas_call(
        functools.partial(finish_kernel, log_ratio),
        out_shape=[
            jax.ShapeDtypeStruct(row.shape, jnp.float32),
            jax.ShapeDtypeStruct(cols[0].shape[1:], jnp.float32),
        ],
        compiler_params=pltpu.CompilerParams(vmem_limit_bytes=VMEM),
        name="finish",
    )(*cols, row)


def combine_kernel(counts, *refs):
    pieces, olds = counts
    lse = log_sum(arrived(refs[:pieces]))
    old_refs, out_ref, kept_refs = (
        refs[pieces : pieces + olds], refs[pieces + olds], refs[pieces + olds + 1 :]
    )
    own_ref, kept_ref = (*old_refs, None)[0], (*kept_refs, None)[0]
    send(lse, out_ref, own_ref, kept_ref)


def combine(pieces, copies, own=None, keep=True):
    lines = pieces[0].shape[1:]
    olds = () if own is None else (own,)
    kind = jnp.bfloat16 if olds else jnp.float32
    return pl.pallas_call(
        functools.partial(combine_kernel, (len(pieces), len(olds))),
        out_shape=[
            jax.ShapeDtypeStruct((copies, *lines), kind),
            *[jax.ShapeDtypeStruct(lines, jnp.float32) for _ in range(keep)],
        ],
        compiler_params=pltpu.CompilerParams(vmem_limit_bytes=VMEM),
        name="combine",
    )(*pieces, *olds)


def shards(frames, codes, pattern):
    along, core = CODES
    chips, cores = lax.axis_size(along), lax.axis_size(core)
    chip, half = lax.axis_index(along), lax.axis_index(core)
    code_copies = chips * cores
    turn = 1 - 2 * half

    def crossing(step):
        there = []
        for k in range(chips):
            for c in range(cores):
                there.append((k * cores + c, (k + (1 - 2 * c) * step) % chips * cores + c))
        return there

    near = lax.ppermute(frames, CODES, crossing(1))
    feature_width = codes.shape[1]
    num_blocks = codes.shape[0] // BLK
    frame_count = pattern.shape[0]
    places = {}
    for name, step in (("own", 0), ("near", -turn), ("back", turn), ("far", 2)):
        places[name, 0] = ((chip + step) % chips * cores + half).reshape(1)
        places[name, 1] = ((chip - step) % chips * cores + 1 - half).reshape(1)
    low = (lax.axis_index(CODES) * num_blocks).reshape(1)
    places, low = lax.optimization_barrier((places, low))
    picked, picks = tables(low, pattern)
    picked_t = picks
    codes = codes.reshape(num_blocks, BLK, feature_width)
    frames_total = frame_count * BLK * lax.axis_size(FRAMES)
    codes_total = num_blocks * BLK * lax.axis_size(CODES)
    log_ratio = math.log(frames_total / codes_total)
    made = ()

    def use(made, name, swapped, block):
        return make_tiles(picks, places[name, swapped], (block,), codes, code_copies, made)

    def swap(block):
        return ring_shift(block, core, 1)

    made = use(made, "own", 1, swap(frames))
    late, made = lax.optimization_barrier((frames, made))
    back = lax.ppermute(late, CODES, crossing(-1))
    made = use(made, "own", 0, frames)
    near, made = lax.optimization_barrier((near, made))
    far = lax.ppermute(near, CODES, crossing(1))
    other = swap(near)
    made = use(made, "near", 0, near)
    made = use(made, "near", 1, other)
    back, made = lax.optimization_barrier((back, made))
    other = swap(back)
    made = use(made, "back", 0, back)
    made = use(made, "back", 1, other)
    far, made = lax.optimization_barrier((far, made))
    other = swap(far)
    made = use(made, "far", 0, far)
    made = use(made, "far", 1, other)
    exps, logits, high, lse = made
    first, second = FRAMES

    def exchange(pieces, axes):
        return lax.all_to_all(pieces, axes, 0, 0, tiled=True)

    pieces, row_sent = combine((lse[None],), code_copies)
    rows = (exchange(pieces, CODES),)
    cols = ()
    col_sent = None
    for iteration in range(ITERS):
        last = iteration == ITERS - 1
        pieces, *kept = column_pass(
            picks, rows, high, picked_t, exps, logits, lax.axis_size(first), last
        )
        rows = tuple(kept) or rows
        pieces = exchange(pieces, first)
        pieces, *kept = combine((pieces,), lax.axis_size(second), col_sent, keep=not last)
        col_sent = None if last else kept[0]
        cols = (*cols[:1], exchange(pieces, second))
        if not last:
            keep = iteration < ITERS - 2
            pieces, *kept = row_pass(
                picks, cols, row_sent, high, picked, exps, logits, code_copies, log_ratio, keep
            )
            if keep:
                row_sent, *kept = kept
            cols = tuple(kept) or cols
            rows = (rows[0], exchange(pieces, CODES))
    row_potential, col_potential = finish(cols, rows[0], log_ratio)
    return (row_potential.reshape(-1), col_potential.reshape(-1))


def solution(mesh):
    torus = Mesh(mesh.devices.reshape(4, 8, 4, 2), ("frames_0", "frames_1", "codes_0", "codes_1"))
    placed = (P(FRAMES_CODES, None), P(CODES, None), P(FRAMES, None))

    return jax.shard_map(
        shards, mesh=torus, in_specs=placed, out_specs=(P(FRAMES), P(CODES)), check_vma=False
    )
```

```python
import functools
import math

import jax
import jax.numpy as jnp
from jax import lax
from jax.experimental import pallas as pl
from jax.experimental.pallas import tpu as pltpu
from jax.sharding import Mesh
from jax.sharding import PartitionSpec as P


BLK = 128
GB = 64
CAP = 6
ITERS = 3
PER = 8
STEP = 8
CODES = ("codes_0", "codes_1")
FRAMES = ("frames_0", "frames_1")
FRAMES_CODES = ("frames_0", "frames_1", "codes_0", "codes_1")

NEG_FILL = -1e30
NEG_ROW = -1e29
SMALL = 1e-26
VMEM = 18 * 1024 * 1024


def tiles_kernel(parts, picks, chunk, codes_ref, *refs):
    exp_ref, logit_ref, high_ref, lse_ref = refs[-4:]
    for b in range(PER):
        held = PER // parts
        at = (b % held) * BLK
        block = refs[b // held][at : at + BLK, :] * jnp.bfloat16(2.0)
        first = picks[0, chunk[0] * PER + b]
        chosen, filled = [], []
        for s in range(CAP):
            pick = picks[s, chunk[0] * PER + b]
            chosen.append(codes_ref[jnp.maximum(jnp.where(pick >= 0, pick, first), 0)])
            filled.append(jnp.where(pick >= 0, 1.0, 0.0))
        top = None
        for s in range(0, CAP, 3):
            three = lax.dot_general(
                jnp.concatenate(chosen[s : s + 3], axis=0),
                block,
                (((1,), (1,)), ((), ())),
                preferred_element_type=jnp.float32,
            )
            logit_ref[b, s * BLK : (s + 3) * BLK, :] = three.astype(jnp.bfloat16)
            part = jnp.max(three.reshape(3 * BLK // 8, 8, BLK), axis=0)
            top = part if top is None else jnp.maximum(top, part)
        high = jnp.max(top, axis=0, keepdims=True).astype(jnp.bfloat16).astype(jnp.float32)
        total = None
        for s in range(CAP):
            tile = logit_ref[b, s * BLK : (s + 1) * BLK, :].astype(jnp.float32)
            terms = jnp.exp(tile - high)
            exp_ref[b, s * BLK : (s + 1) * BLK, :] = terms.astype(jnp.bfloat16)
            part = jnp.sum(terms.reshape(BLK // 8, 8, BLK), axis=0) * filled[s]
            total = part if total is None else total + part
        total = jnp.sum(total, axis=0, keepdims=True)
        high_ref[b : b + 1, :] = jnp.where(first >= 0, high, NEG_ROW)
        lse_ref[b : b + 1, :] = jnp.where(first >= 0, high + jnp.log(total), NEG_FILL)


def make_tiles(picks, chunk, frames, codes, chunks, before):
    parts = len(frames)
    tile_rows = CAP * BLK
    tiles = pl.BlockSpec((PER, tile_rows, BLK), lambda g, _, chunk: (chunk[0], 0, 0))
    lines = pl.BlockSpec((PER, BLK), lambda g, _, chunk: (chunk[0], 0))
    tiles_shape = jax.ShapeDtypeStruct((chunks * PER, tile_rows, BLK), jnp.bfloat16)
    lines_shape = jax.ShapeDtypeStruct((chunks * PER, BLK), jnp.float32)
    return pl.pallas_call(
        functools.partial(tiles_kernel, parts),
        grid_spec=pltpu.PrefetchScalarGridSpec(
            num_scalar_prefetch=2,
            grid=(1,),
            in_specs=[
                pl.BlockSpec(codes.shape, lambda g, *_: (0, 0, 0), pipeline_mode=pl.Buffered(1)),
                *[
                    pl.BlockSpec(part.shape, lambda g, *_: (0, 0), pipeline_mode=pl.Buffered(1))
                    for part in frames
                ],
                *[pl.BlockSpec(memory_space=pl.ANY) for _ in before],
            ],
            out_specs=[tiles, tiles, lines, lines],
        ),
        out_shape=[tiles_shape, tiles_shape, lines_shape, lines_shape],
        input_output_aliases={3 + parts + k: k for k in range(len(before))},
        cost_estimate=pl.CostEstimate(
            flops=2 * tile_rows * PER * BLK * codes.shape[2],
            bytes_accessed=4 * tile_rows * PER * BLK,
            transcendentals=tile_rows * PER * BLK,
        ),
        compiler_params=pltpu.CompilerParams(vmem_limit_bytes=VMEM),
        name="make_tiles",
    )(picks, chunk, codes, *frames, *before)


def pair(tiles_ref, q):
    return jnp.concatenate([tiles_ref[2 * q], tiles_ref[2 * q + 1]], axis=1)


def log_sum(pieces):
    high = pieces[0]
    for piece in pieces[1:]:
        high = jnp.maximum(high, piece)
    total = jnp.exp(pieces[0] - high)
    for piece in pieces[1:]:
        total = total + jnp.exp(piece - high)
    return high + jnp.log(total)


def arrived(refs, kept_ref=None, base=0.0):
    pieces = []
    for k in range(refs[0].shape[0]):
        piece = refs[-1][k].astype(jnp.float32)
        piece = piece + (refs[0][k] if len(refs) == 2 else base)
        pieces.append(piece)
        if kept_ref is not None:
            kept_ref[k] = piece
    return pieces


def send(piece, out_ref, own_ref=None, kept_ref=None, base=0.0):
    before = base if own_ref is None else own_ref[...]
    change = (piece - before).astype(out_ref.dtype)
    if kept_ref is not None:
        kept_ref[...] = before + change.astype(jnp.float32)
    for k in range(out_ref.shape[0]):
        out_ref[k] = change


def split_dot(selector, values):
    upper = values.astype(jnp.bfloat16)
    lower = (values - upper.astype(jnp.float32)).astype(jnp.bfloat16)
    return jnp.dot(selector, upper, preferred_element_type=jnp.float32) + jnp.dot(
        selector, lower, preferred_element_type=jnp.float32
    )


def stable_pass(picks, logit_ref, shift_ref, out_ref, block_ref, high_ref, total_ref, by_code):
    high_ref[...] = jnp.full_like(high_ref, NEG_FILL)
    total_ref[...] = jnp.zeros_like(total_ref)

    def one_group(g, _):
        pltpu.sync_copy(logit_ref.at[pl.ds(g * PER, PER)], block_ref)

        def one_tile(index, _):
            b = index // CAP
            s = index - b * CAP
            row = g * PER + b
            pick = picks[s, row]

            @pl.when(pick >= 0)
            def _():
                rows = pl.ds(pl.multiple_of(s * BLK, BLK), BLK)
                tile = block_ref[b, rows, :].astype(jnp.float32)
                if by_code:
                    tile = jnp.transpose(tile + shift_ref[pl.ds(row, 1), :])
                    at = pl.ds(pick, 1)
                else:
                    shift = jnp.broadcast_to(shift_ref[pl.ds(pick, 1), :], (BLK, BLK))
                    tile = tile + jnp.transpose(shift)
                    at = pl.ds(row, 1)
                before = high_ref[at, :]
                high = jnp.maximum(before, jnp.max(tile, axis=0, keepdims=True))
                total_ref[at, :] = total_ref[at, :] * jnp.exp(before - high) + jnp.sum(
                    jnp.exp(tile - high), axis=0, keepdims=True
                )
                high_ref[at, :] = high

            return 0

        lax.fori_loop(0, CAP * PER, one_tile, 0)
        return 0

    lax.fori_loop(0, logit_ref.shape[0] // PER, one_group, 0)
    total = total_ref[...]
    out_ref[...] = jnp.where(
        total > 0.0, high_ref[...] + jnp.log(jnp.maximum(total, 1e-37)), NEG_FILL
    )


def column_kernel(pieces, last, picks, *refs):
    piece_refs, (high_ref, picks_ref, exp_ref, logit_ref, out_ref), refs = (
        refs[:pieces], refs[pieces : pieces + 5], refs[pieces + 5 :]
    )
    kept_ref = refs[0] if pieces == 2 and not last else None
    row_ref, scale_ref, sums_ref, peak_ref, lse_ref, block_ref, top_ref, total_ref = refs[-8:]
    if last:
        row_ref = refs[0]
    group = pl.program_id(0)

    @pl.when(group == 0)
    def _():
        row = -log_sum(arrived(piece_refs, kept_ref))
        row_ref[...] = row
        weight = high_ref[...] + row
        peak = jnp.max(weight)
        peak_ref[0] = peak
        scale_ref[...] = jnp.exp(weight - peak)

    for part in range(STEP):
        at = pl.ds(pl.multiple_of((group * STEP + part) * PER, PER), PER)
        wide = jnp.concatenate([scale_ref[at, :]] * PER, axis=1)
        lane_block = lax.broadcasted_iota(jnp.int32, wide.shape, 1) // BLK
        row_block = lax.broadcasted_iota(jnp.int32, wide.shape, 0)
        wide = jnp.where(lane_block == row_block, wide, 0.0).astype(jnp.bfloat16)
        sums = None
        for q in range(PER // 2):
            product = lax.dot_general(
                wide[:, 2 * q * BLK : 2 * (q + 1) * BLK],
                pair(exp_ref, part * PER // 2 + q),
                (((1,), (1,)), ((), ())),
                preferred_element_type=jnp.float32,
            )
            sums = product if sums is None else sums + product
        sums_ref[at, :] = sums

    @pl.when(group == pl.num_programs(0) - 1)
    def _():
        blocks = lax.broadcasted_iota(jnp.int32, (GB, picks_ref.shape[1]), 0)
        total = jnp.zeros(lse_ref.shape, jnp.float32)
        used = jnp.zeros((GB, 1), jnp.float32)
        for s in range(CAP):
            hit = (picks_ref[s : s + 1, :] == blocks).astype(jnp.float32)
            used = used + jnp.sum(hit, axis=1, keepdims=True)
            total = total + split_dot(
                hit.astype(jnp.bfloat16), sums_ref[:, s * BLK : (s + 1) * BLK]
            )
        lse_ref[...] = jnp.where(
            total > 0.0, peak_ref[0] + jnp.log(jnp.maximum(total, 1e-37)), NEG_FILL
        )
        low = jnp.min(jnp.where(used > 0.0, total, 1.0))

        @pl.when(jnp.logical_not(low >= SMALL))
        def _():
            stable_pass(
                picks, logit_ref, row_ref, lse_ref, block_ref, top_ref, total_ref, True
            )

        send(lse_ref[...], out_ref)


def row_kernel(pieces, keep, log_ratio, base, picks, *refs):
    piece_refs, (own_ref, high_ref, picks_ref, exp_ref, logit_ref, out_ref), refs = (
        refs[:pieces], refs[pieces : pieces + 6], refs[pieces + 6 :]
    )
    sent_ref = refs[0] if keep else None
    kept_ref = refs[keep]
    col_ref, scale_ref, sums_ref, peak_ref, lse_ref, block_ref, top_ref, total_ref = refs[-8:]
    group = pl.program_id(0)

    @pl.when(group == 0)
    def _():
        col = log_ratio - log_sum(arrived(piece_refs, kept_ref, base))
        col_ref[...] = col
        peak = jnp.max(col)
        peak_ref[0] = peak
        scale = jnp.exp(col - peak).astype(jnp.bfloat16)
        blocks = lax.broadcasted_iota(jnp.int32, (picks_ref.shape[0], GB), 1)
        for s in range(CAP):
            hit = (picks_ref[:, s : s + 1] == blocks).astype(jnp.float32).astype(jnp.bfloat16)
            scale_ref[:, s * BLK : (s + 1) * BLK] = jnp.dot(
                hit, scale, preferred_element_type=jnp.float32
            )

    for part in range(STEP):
        at = pl.ds(pl.multiple_of((group * STEP + part) * PER, PER), PER)
        scale = scale_ref[at, :].astype(jnp.bfloat16)
        row_block = lax.broadcasted_iota(jnp.int32, (PER, BLK), 0)
        total = jnp.zeros((PER, BLK), jnp.float32)
        for q in range(PER // 2):
            wide = jnp.dot(
                scale, pair(exp_ref, part * PER // 2 + q), preferred_element_type=jnp.float32
            )
            total = total + jnp.where(row_block == 2 * q, wide[:, :BLK], 0.0)
            total = total + jnp.where(row_block == 2 * q + 1, wide[:, BLK:], 0.0)
        sums_ref[at, :] = total

    @pl.when(group == pl.num_programs(0) - 1)
    def _():
        total = sums_ref[...]
        lse_ref[...] = jnp.where(
            total > 0.0,
            high_ref[...] + (peak_ref[0] + jnp.log(jnp.maximum(total, 1e-37))),
            NEG_FILL,
        )
        low = jnp.min(jnp.where(picks_ref[:, 0:1] >= 0, total, 1.0))

        @pl.when(jnp.logical_not(low >= SMALL))
        def _():
            stable_pass(
                picks, logit_ref, col_ref, lse_ref, block_ref, top_ref, total_ref, False
            )

        send(lse_ref[...], out_ref, own_ref, sent_ref)


def whole(array):
    zeros = (0,) * array.ndim
    return pl.BlockSpec(array.shape, lambda g, _: zeros, pipeline_mode=pl.Buffered(1))


def fixed(shape):
    zeros = (0,) * len(shape)
    return pl.BlockSpec(shape, lambda g, _: zeros)


def column_pass(picks, pieces, high, picks_t, exps, logits, copies, last):
    groups = exps.shape[0] // PER
    rows = high.shape[0]
    kept = pieces[:1] if len(pieces) == 2 else ()
    if last:
        kept = (high,)
    outs = [
        jax.ShapeDtypeStruct((copies, GB, BLK), jnp.float32),
        *[jax.ShapeDtypeStruct(piece.shape, piece.dtype) for piece in kept],
    ]
    return pl.pallas_call(
        functools.partial(column_kernel, len(pieces), last),
        grid_spec=pltpu.PrefetchScalarGridSpec(
            num_scalar_prefetch=1,
            grid=(groups // STEP,),
            in_specs=[
                *[whole(piece) for piece in pieces],
                whole(high),
                whole(picks_t),
                pl.BlockSpec((STEP * PER, *exps.shape[1:]), lambda g, _: (g, 0, 0)),
                pl.BlockSpec(memory_space=pl.ANY),
            ],
            out_specs=[fixed(out.shape) for out in outs],
            scratch_shapes=[
                pltpu.VMEM((rows, BLK), jnp.float32),
                pltpu.VMEM((rows, BLK), jnp.float32),
                pltpu.VMEM((rows, CAP * BLK), jnp.float32),
                pltpu.SMEM((1,), jnp.float32),
                pltpu.VMEM((GB, BLK), jnp.float32),
                pltpu.VMEM((PER, *exps.shape[1:]), jnp.bfloat16),
                pltpu.VMEM((GB, BLK), jnp.float32),
                pltpu.VMEM((GB, BLK), jnp.float32),
            ],
        ),
        out_shape=outs,
        compiler_params=pltpu.CompilerParams(vmem_limit_bytes=VMEM),
        name="column_pass",
    )(picks, *pieces, high, picks_t, exps, logits)


def row_pass(picks, pieces, own, high, picks_v, exps, logits, copies, log_ratio, base, keep):
    groups = exps.shape[0] // PER
    rows = high.shape[0]
    outs = [
        jax.ShapeDtypeStruct((copies, rows, BLK), jnp.bfloat16),
        *[jax.ShapeDtypeStruct((rows, BLK), jnp.float32) for _ in range(keep)],
        jax.ShapeDtypeStruct(pieces[0].shape, jnp.float32),
    ]
    return pl.pallas_call(
        functools.partial(row_kernel, len(pieces), keep, log_ratio, base),
        grid_spec=pltpu.PrefetchScalarGridSpec(
            num_scalar_prefetch=1,
            grid=(groups // STEP,),
            in_specs=[
                *[whole(piece) for piece in pieces],
                whole(own),
                whole(high),
                whole(picks_v),
                pl.BlockSpec((STEP * PER, *exps.shape[1:]), lambda g, _: (g, 0, 0)),
                pl.BlockSpec(memory_space=pl.ANY),
            ],
            out_specs=[fixed(out.shape) for out in outs],
            scratch_shapes=[
                pltpu.VMEM((GB, BLK), jnp.float32),
                pltpu.VMEM((rows, CAP * BLK), jnp.float32),
                pltpu.VMEM((rows, BLK), jnp.float32),
                pltpu.SMEM((1,), jnp.float32),
                pltpu.VMEM((rows, BLK), jnp.float32),
                pltpu.VMEM((PER, *exps.shape[1:]), jnp.bfloat16),
                pltpu.VMEM((rows, BLK), jnp.float32),
                pltpu.VMEM((rows, BLK), jnp.float32),
            ],
        ),
        out_shape=outs,
        compiler_params=pltpu.CompilerParams(vmem_limit_bytes=VMEM),
        name="row_pass",
    )(picks, *pieces, own, high, picks_v, exps, logits)


def tables_kernel(low_ref, pattern_ref, picked_ref, table_ref):
    low = low_ref[0]
    pattern = pattern_ref[...]
    rows, slots = pattern.shape
    first = jnp.sum(jnp.where(pattern < low, 1.0, 0.0), axis=1, keepdims=True)
    position = lax.broadcasted_iota(jnp.int32, (rows, slots), 1).astype(jnp.float32) - first
    offset = (pattern - low).astype(jnp.float32)
    lane = lax.broadcasted_iota(jnp.int32, (rows, BLK), 1)
    picked = jnp.full((rows, BLK), -1.0, jnp.float32)
    for s in range(CAP):
        found = jnp.max(jnp.where(position == s, offset, -1.0), axis=1, keepdims=True)
        found = jnp.where(found < GB, found, -1.0)
        picked = jnp.where(lane == s, found, picked)
    picked_ref[...] = picked[:, :8].astype(jnp.int32)
    table_ref[...] = jnp.transpose(picked)[:8, :].astype(jnp.int32)


def tables(low, pattern):
    rows = pattern.shape[0]
    near = pl.BlockSpec(memory_space=pltpu.VMEM)
    return pl.pallas_call(
        tables_kernel,
        in_specs=[pl.BlockSpec(memory_space=pltpu.SMEM), near],
        out_specs=[near, near],
        out_shape=[
            jax.ShapeDtypeStruct((rows, 8), jnp.int32),
            jax.ShapeDtypeStruct((8, rows), jnp.int32),
        ],
        cost_estimate=pl.CostEstimate(flops=0, bytes_accessed=1 << 23, transcendentals=0),
        compiler_params=pltpu.CompilerParams(vmem_limit_bytes=VMEM),
        name="tables",
    )(low, pattern)


def ring_shift(array, axis, step):
    size = lax.axis_size(axis)
    return lax.ppermute(array, axis, [(k, (k + step) % size) for k in range(size)])


def finish_kernel(log_ratio, kept_ref, change_ref, row_ref, row_out_ref, col_out_ref):
    row_out_ref[...] = row_ref[...]
    col_out_ref[...] = log_ratio - log_sum(arrived((kept_ref, change_ref)))


def finish(cols, row, log_ratio):
    return pl.pallas_call(
        functools.partial(finish_kernel, log_ratio),
        out_shape=[
            jax.ShapeDtypeStruct(row.shape, jnp.float32),
            jax.ShapeDtypeStruct(cols[0].shape[1:], jnp.float32),
        ],
        compiler_params=pltpu.CompilerParams(vmem_limit_bytes=VMEM),
        name="finish",
    )(*cols, row)


def combine_kernel(olds, base, pieces_ref, *refs):
    own_ref = refs[0] if olds else None
    kept_ref = (*refs[olds + 1 :], None)[0]
    send(log_sum(arrived((pieces_ref,))), refs[olds], own_ref, kept_ref, base)


def combine(pieces, copies, own=None, keep=True, base=0.0, kind=jnp.bfloat16):
    lines = pieces.shape[1:]
    olds = () if own is None else (own,)
    return pl.pallas_call(
        functools.partial(combine_kernel, len(olds), base),
        out_shape=[
            jax.ShapeDtypeStruct((copies, *lines), kind),
            *[jax.ShapeDtypeStruct(lines, jnp.float32) for _ in range(keep)],
        ],
        compiler_params=pltpu.CompilerParams(vmem_limit_bytes=VMEM),
        name="combine",
    )(pieces, *olds)


def shards(frames, codes, pattern):
    along, core = CODES
    chips, cores = lax.axis_size(along), lax.axis_size(core)
    chip, half = lax.axis_index(along), lax.axis_index(core)
    code_copies = chips * cores
    turn = 1 - 2 * half

    def crossing(step):
        there = []
        for k in range(chips):
            for c in range(cores):
                there.append((k * cores + c, (k + (1 - 2 * c) * step) % chips * cores + c))
        return there

    near = lax.ppermute(frames, CODES, crossing(1))
    feature_width = codes.shape[1]
    num_blocks = codes.shape[0] // BLK
    frame_count = pattern.shape[0]
    places = {}
    for name, step in (("own", 0), ("near", -turn), ("back", turn), ("far", 2)):
        places[name, 0] = ((chip + step) % chips * cores + half).reshape(1)
        places[name, 1] = ((chip - step) % chips * cores + 1 - half).reshape(1)
    low = (lax.axis_index(CODES) * num_blocks).reshape(1)
    places, low = lax.optimization_barrier((places, low))
    picked, picks = tables(low, pattern)
    picked_t = picks
    codes = codes.reshape(num_blocks, BLK, feature_width)
    frames_total = frame_count * BLK * lax.axis_size(FRAMES)
    codes_total = num_blocks * BLK * lax.axis_size(CODES)
    log_ratio = math.log(frames_total / codes_total)
    made = ()

    def use(made, name, swapped, block):
        return make_tiles(picks, places[name, swapped], (block,), codes, code_copies, made)

    def swap(block):
        return ring_shift(block, core, 1)

    made = use(made, "own", 1, swap(frames))
    late, made = lax.optimization_barrier((frames, made))
    back = lax.ppermute(late, CODES, crossing(-1))
    made = use(made, "own", 0, frames)
    near, made = lax.optimization_barrier((near, made))
    far = lax.ppermute(near, CODES, crossing(1))
    other = swap(near)
    made = use(made, "near", 0, near)
    made = use(made, "near", 1, other)
    back, made = lax.optimization_barrier((back, made))
    other = swap(back)
    made = use(made, "back", 0, back)
    made = use(made, "back", 1, other)
    far, made = lax.optimization_barrier((far, made))
    other = swap(far)
    made = use(made, "far", 0, far)
    made = use(made, "far", 1, other)
    exps, logits, high, lse = made
    first, second = FRAMES

    def exchange(pieces, axes):
        return lax.all_to_all(pieces, axes, 0, 0, tiled=True)

    base = log_ratio - math.log(lax.axis_size(second))
    pieces, row_sent = combine(lse[None], code_copies, kind=jnp.float32)
    rows = (exchange(pieces, CODES),)
    cols = ()
    col_sent = None
    for iteration in range(ITERS):
        last = iteration == ITERS - 1
        pieces, *kept = column_pass(
            picks, rows, high, picked_t, exps, logits, lax.axis_size(first), last
        )
        rows = tuple(kept) or rows
        pieces = exchange(pieces, first)
        pieces, *kept = combine(pieces, lax.axis_size(second), col_sent, not last, base)
        col_sent = None if last else kept[0]
        cols = (*cols, exchange(pieces, second))
        if not last:
            keep = iteration < ITERS - 2
            pieces, *kept = row_pass(
                picks, cols, row_sent, high, picked, exps, logits, code_copies, log_ratio, base, keep
            )
            if keep:
                row_sent, *kept = kept
            cols = tuple(kept)
            rows = (rows[0], exchange(pieces, CODES))
    row_potential, col_potential = finish(cols, rows[0], log_ratio)
    return (row_potential.reshape(-1), col_potential.reshape(-1))


def solution(mesh):
    torus = Mesh(mesh.devices.reshape(4, 8, 4, 2), ("frames_0", "frames_1", "codes_0", "codes_1"))
    placed = (P(FRAMES_CODES, None), P(CODES, None), P(FRAMES, None))

    return jax.shard_map(
        shards, mesh=torus, in_specs=placed, out_specs=(P(FRAMES), P(CODES)), check_vma=False
    )
```

```python
import functools
import math

import jax
import jax.numpy as jnp
from jax import lax
from jax.experimental import pallas as pl
from jax.experimental.pallas import tpu as pltpu
from jax.sharding import Mesh
from jax.sharding import PartitionSpec as P


BLK = 128
GB = 64
CAP = 6
ITERS = 3
PER = 8
STEP = 8
CODES = ("codes_0", "codes_1")
FRAMES = ("frames_0", "frames_1")
FRAMES_CODES = ("frames_0", "frames_1", "codes_0", "codes_1")

NEG_FILL = -1e30
NEG_ROW = -1e29
SMALL = 1e-26
VMEM = 18 * 1024 * 1024


def tiles_kernel(parts, picks, chunk, codes_ref, *refs):
    exp_ref, logit_ref, high_ref, lse_ref = refs[-4:]
    for b in range(PER):
        held = PER // parts
        at = (b % held) * BLK
        block = refs[b // held][at : at + BLK, :] * jnp.bfloat16(2.0)
        first = picks[0, chunk[0] * PER + b]
        chosen, filled = [], []
        for s in range(CAP):
            pick = picks[s, chunk[0] * PER + b]
            chosen.append(codes_ref[jnp.maximum(jnp.where(pick >= 0, pick, first), 0)])
            filled.append(jnp.where(pick >= 0, 1.0, 0.0))
        top = None
        for s in range(0, CAP, 3):
            three = lax.dot_general(
                jnp.concatenate(chosen[s : s + 3], axis=0),
                block,
                (((1,), (1,)), ((), ())),
                preferred_element_type=jnp.float32,
            )
            three = three.astype(jnp.bfloat16)
            logit_ref[b, s * BLK : (s + 3) * BLK, :] = three
            part = jnp.max(three.reshape(3 * BLK // 16, 16, BLK), axis=0)
            top = part if top is None else jnp.maximum(top, part)
        high = jnp.max(top.astype(jnp.float32), axis=0, keepdims=True)
        total = None
        for s in range(CAP):
            tile = logit_ref[b, s * BLK : (s + 1) * BLK, :].astype(jnp.float32)
            terms = jnp.exp(tile - high)
            exp_ref[b, s * BLK : (s + 1) * BLK, :] = terms.astype(jnp.bfloat16)
            part = jnp.sum(terms.reshape(BLK // 8, 8, BLK), axis=0) * filled[s]
            total = part if total is None else total + part
        total = jnp.sum(total, axis=0, keepdims=True)
        high_ref[b : b + 1, :] = jnp.where(first >= 0, high, NEG_ROW)
        lse_ref[b : b + 1, :] = jnp.where(first >= 0, high + jnp.log(total), NEG_FILL)


def make_tiles(picks, chunk, frames, codes, chunks, before):
    parts = len(frames)
    tile_rows = CAP * BLK
    tiles = pl.BlockSpec((PER, tile_rows, BLK), lambda g, _, chunk: (chunk[0], 0, 0))
    lines = pl.BlockSpec((PER, BLK), lambda g, _, chunk: (chunk[0], 0))
    tiles_shape = jax.ShapeDtypeStruct((chunks * PER, tile_rows, BLK), jnp.bfloat16)
    lines_shape = jax.ShapeDtypeStruct((chunks * PER, BLK), jnp.float32)
    return pl.pallas_call(
        functools.partial(tiles_kernel, parts),
        grid_spec=pltpu.PrefetchScalarGridSpec(
            num_scalar_prefetch=2,
            grid=(1,),
            in_specs=[
                pl.BlockSpec(codes.shape, lambda g, *_: (0, 0, 0), pipeline_mode=pl.Buffered(1)),
                *[
                    pl.BlockSpec(part.shape, lambda g, *_: (0, 0), pipeline_mode=pl.Buffered(1))
                    for part in frames
                ],
                *[pl.BlockSpec(memory_space=pl.ANY) for _ in before],
            ],
            out_specs=[tiles, tiles, lines, lines],
        ),
        out_shape=[tiles_shape, tiles_shape, lines_shape, lines_shape],
        input_output_aliases={3 + parts + k: k for k in range(len(before))},
        cost_estimate=pl.CostEstimate(
            flops=2 * tile_rows * PER * BLK * codes.shape[2],
            bytes_accessed=4 * tile_rows * PER * BLK,
            transcendentals=tile_rows * PER * BLK,
        ),
        compiler_params=pltpu.CompilerParams(vmem_limit_bytes=VMEM),
        name="make_tiles",
    )(picks, chunk, codes, *frames, *before)


def pair(tiles_ref, q):
    return jnp.concatenate([tiles_ref[2 * q], tiles_ref[2 * q + 1]], axis=1)


def log_sum(pieces):
    high = pieces[0]
    for piece in pieces[1:]:
        high = jnp.maximum(high, piece)
    total = jnp.exp(pieces[0] - high)
    for piece in pieces[1:]:
        total = total + jnp.exp(piece - high)
    return high + jnp.log(total)


def arrived(refs, kept_ref=None, base=0.0):
    pieces = []
    for k in range(refs[0].shape[0]):
        piece = refs[-1][k].astype(jnp.float32)
        piece = piece + (refs[0][k] if len(refs) == 2 else base)
        pieces.append(piece)
        if kept_ref is not None:
            kept_ref[k] = piece
    return pieces


def send(piece, out_ref, own_ref=None, kept_ref=None, base=0.0):
    before = base if own_ref is None else own_ref[...]
    change = (piece - before).astype(out_ref.dtype)
    if kept_ref is not None:
        kept_ref[...] = before + change.astype(jnp.float32)
    for k in range(out_ref.shape[0]):
        out_ref[k] = change


def split_dot(selector, values):
    upper = values.astype(jnp.bfloat16)
    lower = (values - upper.astype(jnp.float32)).astype(jnp.bfloat16)
    return jnp.dot(selector, upper, preferred_element_type=jnp.float32) + jnp.dot(
        selector, lower, preferred_element_type=jnp.float32
    )


def stable_pass(picks, logit_ref, shift_ref, out_ref, block_ref, high_ref, total_ref, by_code):
    high_ref[...] = jnp.full_like(high_ref, NEG_FILL)
    total_ref[...] = jnp.zeros_like(total_ref)

    def one_group(g, _):
        pltpu.sync_copy(logit_ref.at[pl.ds(g * PER, PER)], block_ref)

        def one_tile(index, _):
            b = index // CAP
            s = index - b * CAP
            row = g * PER + b
            pick = picks[s, row]

            @pl.when(pick >= 0)
            def _():
                rows = pl.ds(pl.multiple_of(s * BLK, BLK), BLK)
                tile = block_ref[b, rows, :].astype(jnp.float32)
                if by_code:
                    tile = jnp.transpose(tile + shift_ref[pl.ds(row, 1), :])
                    at = pl.ds(pick, 1)
                else:
                    shift = jnp.broadcast_to(shift_ref[pl.ds(pick, 1), :], (BLK, BLK))
                    tile = tile + jnp.transpose(shift)
                    at = pl.ds(row, 1)
                before = high_ref[at, :]
                high = jnp.maximum(before, jnp.max(tile, axis=0, keepdims=True))
                total_ref[at, :] = total_ref[at, :] * jnp.exp(before - high) + jnp.sum(
                    jnp.exp(tile - high), axis=0, keepdims=True
                )
                high_ref[at, :] = high

            return 0

        lax.fori_loop(0, CAP * PER, one_tile, 0)
        return 0

    lax.fori_loop(0, logit_ref.shape[0] // PER, one_group, 0)
    total = total_ref[...]
    out_ref[...] = jnp.where(
        total > 0.0, high_ref[...] + jnp.log(jnp.maximum(total, 1e-37)), NEG_FILL
    )


def column_kernel(pieces, last, picks, *refs):
    piece_refs, (high_ref, picks_ref, exp_ref, logit_ref, out_ref), refs = (
        refs[:pieces], refs[pieces : pieces + 5], refs[pieces + 5 :]
    )
    kept_ref = refs[0] if pieces == 2 and not last else None
    row_ref, scale_ref, sums_ref, peak_ref, lse_ref, block_ref, top_ref, total_ref = refs[-8:]
    if last:
        row_ref = refs[0]
    group = pl.program_id(0)

    @pl.when(group == 0)
    def _():
        row = -log_sum(arrived(piece_refs, kept_ref))
        row_ref[...] = row
        weight = high_ref[...] + row
        peak = jnp.max(weight)
        peak_ref[0] = peak
        scale_ref[...] = jnp.exp(weight - peak)

    for part in range(STEP):
        at = pl.ds(pl.multiple_of((group * STEP + part) * PER, PER), PER)
        wide = jnp.concatenate([scale_ref[at, :]] * PER, axis=1)
        lane_block = lax.broadcasted_iota(jnp.int32, wide.shape, 1) // BLK
        row_block = lax.broadcasted_iota(jnp.int32, wide.shape, 0)
        wide = jnp.where(lane_block == row_block, wide, 0.0).astype(jnp.bfloat16)
        sums = None
        for q in range(PER // 2):
            product = lax.dot_general(
                wide[:, 2 * q * BLK : 2 * (q + 1) * BLK],
                pair(exp_ref, part * PER // 2 + q),
                (((1,), (1,)), ((), ())),
                preferred_element_type=jnp.float32,
            )
            sums = product if sums is None else sums + product
        sums_ref[at, :] = sums

    @pl.when(group == pl.num_programs(0) - 1)
    def _():
        blocks = lax.broadcasted_iota(jnp.int32, (GB, picks_ref.shape[1]), 0)
        total = jnp.zeros(lse_ref.shape, jnp.float32)
        used = jnp.zeros((GB, 1), jnp.float32)
        for s in range(CAP):
            hit = (picks_ref[s : s + 1, :] == blocks).astype(jnp.float32)
            used = used + jnp.sum(hit, axis=1, keepdims=True)
            total = total + split_dot(
                hit.astype(jnp.bfloat16), sums_ref[:, s * BLK : (s + 1) * BLK]
            )
        lse_ref[...] = jnp.where(
            total > 0.0, peak_ref[0] + jnp.log(jnp.maximum(total, 1e-37)), NEG_FILL
        )
        low = jnp.min(jnp.where(used > 0.0, total, 1.0))

        @pl.when(jnp.logical_not(low >= SMALL))
        def _():
            stable_pass(
                picks, logit_ref, row_ref, lse_ref, block_ref, top_ref, total_ref, True
            )

        send(lse_ref[...], out_ref)


def row_kernel(pieces, keep, log_ratio, base, picks, *refs):
    piece_refs, (own_ref, high_ref, picks_ref, exp_ref, logit_ref, out_ref), refs = (
        refs[:pieces], refs[pieces : pieces + 6], refs[pieces + 6 :]
    )
    sent_ref = refs[0] if keep else None
    kept_ref = refs[keep]
    col_ref, scale_ref, sums_ref, peak_ref, lse_ref, block_ref, top_ref, total_ref = refs[-8:]
    group = pl.program_id(0)

    @pl.when(group == 0)
    def _():
        col = log_ratio - log_sum(arrived(piece_refs, kept_ref, base))
        col_ref[...] = col
        peak = jnp.max(col)
        peak_ref[0] = peak
        scale = jnp.exp(col - peak).astype(jnp.bfloat16)
        blocks = lax.broadcasted_iota(jnp.int32, (picks_ref.shape[0], GB), 1)
        for s in range(CAP):
            hit = (picks_ref[:, s : s + 1] == blocks).astype(jnp.float32).astype(jnp.bfloat16)
            scale_ref[:, s * BLK : (s + 1) * BLK] = jnp.dot(
                hit, scale, preferred_element_type=jnp.float32
            )

    for part in range(STEP):
        at = pl.ds(pl.multiple_of((group * STEP + part) * PER, PER), PER)
        scale = scale_ref[at, :].astype(jnp.bfloat16)
        row_block = lax.broadcasted_iota(jnp.int32, (PER, BLK), 0)
        total = jnp.zeros((PER, BLK), jnp.float32)
        for q in range(PER // 2):
            wide = jnp.dot(
                scale, pair(exp_ref, part * PER // 2 + q), preferred_element_type=jnp.float32
            )
            total = total + jnp.where(row_block == 2 * q, wide[:, :BLK], 0.0)
            total = total + jnp.where(row_block == 2 * q + 1, wide[:, BLK:], 0.0)
        sums_ref[at, :] = total

    @pl.when(group == pl.num_programs(0) - 1)
    def _():
        total = sums_ref[...]
        lse_ref[...] = jnp.where(
            total > 0.0,
            high_ref[...] + (peak_ref[0] + jnp.log(jnp.maximum(total, 1e-37))),
            NEG_FILL,
        )
        low = jnp.min(jnp.where(picks_ref[:, 0:1] >= 0, total, 1.0))

        @pl.when(jnp.logical_not(low >= SMALL))
        def _():
            stable_pass(
                picks, logit_ref, col_ref, lse_ref, block_ref, top_ref, total_ref, False
            )

        send(lse_ref[...], out_ref, own_ref, sent_ref)


def whole(array):
    zeros = (0,) * array.ndim
    return pl.BlockSpec(array.shape, lambda g, _: zeros, pipeline_mode=pl.Buffered(1))


def fixed(shape):
    zeros = (0,) * len(shape)
    return pl.BlockSpec(shape, lambda g, _: zeros)


def column_pass(picks, pieces, high, picks_t, exps, logits, copies, last):
    groups = exps.shape[0] // PER
    rows = high.shape[0]
    kept = pieces[:1] if len(pieces) == 2 else ()
    if last:
        kept = (high,)
    outs = [
        jax.ShapeDtypeStruct((copies, GB, BLK), jnp.float32),
        *[jax.ShapeDtypeStruct(piece.shape, piece.dtype) for piece in kept],
    ]
    return pl.pallas_call(
        functools.partial(column_kernel, len(pieces), last),
        grid_spec=pltpu.PrefetchScalarGridSpec(
            num_scalar_prefetch=1,
            grid=(groups // STEP,),
            in_specs=[
                *[whole(piece) for piece in pieces],
                whole(high),
                whole(picks_t),
                pl.BlockSpec((STEP * PER, *exps.shape[1:]), lambda g, _: (g, 0, 0)),
                pl.BlockSpec(memory_space=pl.ANY),
            ],
            out_specs=[fixed(out.shape) for out in outs],
            scratch_shapes=[
                pltpu.VMEM((rows, BLK), jnp.float32),
                pltpu.VMEM((rows, BLK), jnp.float32),
                pltpu.VMEM((rows, CAP * BLK), jnp.float32),
                pltpu.SMEM((1,), jnp.float32),
                pltpu.VMEM((GB, BLK), jnp.float32),
                pltpu.VMEM((PER, *exps.shape[1:]), jnp.bfloat16),
                pltpu.VMEM((GB, BLK), jnp.float32),
                pltpu.VMEM((GB, BLK), jnp.float32),
            ],
        ),
        out_shape=outs,
        compiler_params=pltpu.CompilerParams(vmem_limit_bytes=VMEM),
        name="column_pass",
    )(picks, *pieces, high, picks_t, exps, logits)


def row_pass(picks, pieces, own, high, picks_v, exps, logits, copies, log_ratio, base, keep):
    groups = exps.shape[0] // PER
    rows = high.shape[0]
    outs = [
        jax.ShapeDtypeStruct((copies, rows, BLK), jnp.bfloat16),
        *[jax.ShapeDtypeStruct((rows, BLK), jnp.float32) for _ in range(keep)],
        jax.ShapeDtypeStruct(pieces[0].shape, jnp.float32),
    ]
    return pl.pallas_call(
        functools.partial(row_kernel, len(pieces), keep, log_ratio, base),
        grid_spec=pltpu.PrefetchScalarGridSpec(
            num_scalar_prefetch=1,
            grid=(groups // STEP,),
            in_specs=[
                *[whole(piece) for piece in pieces],
                whole(own),
                whole(high),
                whole(picks_v),
                pl.BlockSpec((STEP * PER, *exps.shape[1:]), lambda g, _: (g, 0, 0)),
                pl.BlockSpec(memory_space=pl.ANY),
            ],
            out_specs=[fixed(out.shape) for out in outs],
            scratch_shapes=[
                pltpu.VMEM((GB, BLK), jnp.float32),
                pltpu.VMEM((rows, CAP * BLK), jnp.float32),
                pltpu.VMEM((rows, BLK), jnp.float32),
                pltpu.SMEM((1,), jnp.float32),
                pltpu.VMEM((rows, BLK), jnp.float32),
                pltpu.VMEM((PER, *exps.shape[1:]), jnp.bfloat16),
                pltpu.VMEM((rows, BLK), jnp.float32),
                pltpu.VMEM((rows, BLK), jnp.float32),
            ],
        ),
        out_shape=outs,
        compiler_params=pltpu.CompilerParams(vmem_limit_bytes=VMEM),
        name="row_pass",
    )(picks, *pieces, own, high, picks_v, exps, logits)


def tables_kernel(low_ref, pattern_ref, picked_ref, table_ref):
    low = low_ref[0]
    pattern = pattern_ref[...]
    rows, slots = pattern.shape
    first = jnp.sum(jnp.where(pattern < low, 1.0, 0.0), axis=1, keepdims=True)
    position = lax.broadcasted_iota(jnp.int32, (rows, slots), 1).astype(jnp.float32) - first
    offset = (pattern - low).astype(jnp.float32)
    lane = lax.broadcasted_iota(jnp.int32, (rows, BLK), 1)
    picked = jnp.full((rows, BLK), -1.0, jnp.float32)
    for s in range(CAP):
        found = jnp.max(jnp.where(position == s, offset, -1.0), axis=1, keepdims=True)
        found = jnp.where(found < GB, found, -1.0)
        picked = jnp.where(lane == s, found, picked)
    picked_ref[...] = picked[:, :8].astype(jnp.int32)
    table_ref[...] = jnp.transpose(picked)[:8, :].astype(jnp.int32)


def tables(low, pattern):
    rows = pattern.shape[0]
    near = pl.BlockSpec(memory_space=pltpu.VMEM)
    return pl.pallas_call(
        tables_kernel,
        in_specs=[pl.BlockSpec(memory_space=pltpu.SMEM), near],
        out_specs=[near, near],
        out_shape=[
            jax.ShapeDtypeStruct((rows, 8), jnp.int32),
            jax.ShapeDtypeStruct((8, rows), jnp.int32),
        ],
        cost_estimate=pl.CostEstimate(flops=0, bytes_accessed=1 << 23, transcendentals=0),
        compiler_params=pltpu.CompilerParams(vmem_limit_bytes=VMEM),
        name="tables",
    )(low, pattern)


def ring_shift(array, axis, step):
    size = lax.axis_size(axis)
    return lax.ppermute(array, axis, [(k, (k + step) % size) for k in range(size)])


def finish_kernel(log_ratio, kept_ref, change_ref, row_ref, row_out_ref, col_out_ref):
    row_out_ref[...] = row_ref[...]
    col_out_ref[...] = log_ratio - log_sum(arrived((kept_ref, change_ref)))


def finish(cols, row, log_ratio):
    return pl.pallas_call(
        functools.partial(finish_kernel, log_ratio),
        out_shape=[
            jax.ShapeDtypeStruct(row.shape, jnp.float32),
            jax.ShapeDtypeStruct(cols[0].shape[1:], jnp.float32),
        ],
        compiler_params=pltpu.CompilerParams(vmem_limit_bytes=VMEM),
        name="finish",
    )(*cols, row)


def combine_kernel(olds, base, pieces_ref, *refs):
    own_ref = refs[0] if olds else None
    kept_ref = (*refs[olds + 1 :], None)[0]
    send(log_sum(arrived((pieces_ref,))), refs[olds], own_ref, kept_ref, base)


def combine(pieces, copies, own=None, keep=True, base=0.0, kind=jnp.bfloat16):
    lines = pieces.shape[1:]
    olds = () if own is None else (own,)
    return pl.pallas_call(
        functools.partial(combine_kernel, len(olds), base),
        out_shape=[
            jax.ShapeDtypeStruct((copies, *lines), kind),
            *[jax.ShapeDtypeStruct(lines, jnp.float32) for _ in range(keep)],
        ],
        compiler_params=pltpu.CompilerParams(vmem_limit_bytes=VMEM),
        name="combine",
    )(pieces, *olds)


def shards(frames, codes, pattern):
    along, core = CODES
    chips, cores = lax.axis_size(along), lax.axis_size(core)
    chip, half = lax.axis_index(along), lax.axis_index(core)
    code_copies = chips * cores
    turn = 1 - 2 * half

    def crossing(step):
        there = []
        for k in range(chips):
            for c in range(cores):
                there.append((k * cores + c, (k + (1 - 2 * c) * step) % chips * cores + c))
        return there

    near = lax.ppermute(frames, CODES, crossing(1))
    feature_width = codes.shape[1]
    num_blocks = codes.shape[0] // BLK
    frame_count = pattern.shape[0]
    places = {}
    for name, step in (("own", 0), ("near", -turn), ("back", turn), ("far", 2)):
        places[name, 0] = ((chip + step) % chips * cores + half).reshape(1)
        places[name, 1] = ((chip - step) % chips * cores + 1 - half).reshape(1)
    low = (lax.axis_index(CODES) * num_blocks).reshape(1)
    places, low = lax.optimization_barrier((places, low))
    picked, picks = tables(low, pattern)
    picked_t = picks
    codes = codes.reshape(num_blocks, BLK, feature_width)
    frames_total = frame_count * BLK * lax.axis_size(FRAMES)
    codes_total = num_blocks * BLK * lax.axis_size(CODES)
    log_ratio = math.log(frames_total / codes_total)
    made = ()

    def use(made, name, swapped, block):
        return make_tiles(picks, places[name, swapped], (block,), codes, code_copies, made)

    def swap(block):
        return ring_shift(block, core, 1)

    made = use(made, "own", 1, swap(frames))
    late, made = lax.optimization_barrier((frames, made))
    back = lax.ppermute(late, CODES, crossing(-1))
    near, made = lax.optimization_barrier((near, made))
    far = lax.ppermute(near, CODES, crossing(1))
    other = swap(near)
    made = use(made, "near", 0, near)
    made = use(made, "near", 1, other)
    made = use(made, "own", 0, frames)
    back, made = lax.optimization_barrier((back, made))
    other = swap(back)
    made = use(made, "back", 0, back)
    made = use(made, "back", 1, other)
    far, made = lax.optimization_barrier((far, made))
    other = swap(far)
    made = use(made, "far", 0, far)
    made = use(made, "far", 1, other)
    exps, logits, high, lse = made
    first, second = FRAMES

    def exchange(pieces, axes):
        return lax.all_to_all(pieces, axes, 0, 0, tiled=True)

    base = log_ratio - math.log(lax.axis_size(second))
    pieces, row_sent = combine(lse[None], code_copies, kind=jnp.float32)
    rows = (exchange(pieces, CODES),)
    cols = ()
    col_sent = None
    for iteration in range(ITERS):
        last = iteration == ITERS - 1
        pieces, *kept = column_pass(
            picks, rows, high, picked_t, exps, logits, lax.axis_size(first), last
        )
        rows = tuple(kept) or rows
        pieces = exchange(pieces, first)
        pieces, *kept = combine(pieces, lax.axis_size(second), col_sent, not last, base)
        col_sent = None if last else kept[0]
        cols = (*cols, exchange(pieces, second))
        if not last:
            keep = iteration < ITERS - 2
            pieces, *kept = row_pass(
                picks, cols, row_sent, high, picked, exps, logits, code_copies, log_ratio, base, keep
            )
            if keep:
                row_sent, *kept = kept
            cols = tuple(kept)
            rows = (rows[0], exchange(pieces, CODES))
    row_potential, col_potential = finish(cols, rows[0], log_ratio)
    return (row_potential.reshape(-1), col_potential.reshape(-1))


def solution(mesh):
    torus = Mesh(mesh.devices.reshape(4, 8, 4, 2), ("frames_0", "frames_1", "codes_0", "codes_1"))
    placed = (P(FRAMES_CODES, None), P(CODES, None), P(FRAMES, None))

    return jax.shard_map(
        shards, mesh=torus, in_specs=placed, out_specs=(P(FRAMES), P(CODES)), check_vma=False
    )
```
